32 devices in a mesh: grp: 2 (over x), lon: 16 (over z, y, core), lat: 1.
Axes of the slice: x: 2, y: 2, z: 4, core: 2. Of those that a mesh axis runs over, the one named last changes fastest.
Arguments:
- tokens: bfloat16 [4, 8, 128, 1536], P('grp', 'lat', 'lon'), parts along dimension 0, may hold values from -6 to 6
- land: int32 [16, 128], P(('grp', 'lat'), 'lon'), parts along dimension 0, may hold values 0 or 1
- surface: float32 [2, 1536], replicated, may hold values from -4 to 4
- gain: float32 [1536], replicated, may hold values from 0.25 to 1.75
- weights: bfloat16 [1536, 3072], P('lon'), may hold values from -0.15625 to 0.15625
- shifts: int32 [2, 2], replicated, may hold values from 1 to 7, as said below
- index_table: int32 [64, 64], replicated, may hold values from 0 to 224
- bias_table: float32 [2, 225, 12], P('lat'), as said below
- cotangent: bfloat16 [4, 8, 128, 1536], P('grp', 'lat', 'lon'), parts along dimension 0, may hold values from -6 to 6
Outputs:
- output: bfloat16 [4, 8, 128, 1536], P('grp', 'lat', 'lon'), parts along dimension 0
- grad_tokens: bfloat16 [4, 8, 128, 1536], P('grp', 'lat', 'lon'), parts along dimension 0
- grad_weights: float32 [3072, 3072], P(('grp', 'lon')), parts along dimension 0
The draws below stay inside these ranges and needn't reach their ends.
There are 2 independent parts, one for each index of `grp`. The reference program is written for one: setup_inputs(seed, part) draws one part's arguments, and reference() takes and returns one part's arrays. A program takes and returns all parts, laid end to end along the dimension named above; an argument that names none is the same for every part. Nothing has to cross between parts.
Inputs may be any that keep to these rules, and one draw needn't show every extreme that they name: `shifts`: row l holds level l's offsets along latitude and longitude; taken together the entries include 1 and 7. `bias_table`: every entry is finite.
All inputs are finite; a program needn't handle non-finite values. No bound on the sum of `land` on one device may be relied on, other than what follows from the above.
Results may differ from the reference program's by a relative error of at most 0.023.
Values may be sent and summed in bfloat16 or wider, within the bound.
A program may use at most 128 MiB of HBM per device.

```python
import math
import jax
import jax.numpy as jnp
from jax import lax

D = 1536
HEADS = 12
HDIM = 64
WIN = 8
LVL = 2
CLON = 8
HD = 768
NREL = 225
NLAT = 8
NLON = 128
BANDS = 2
N_LON = 16
N_LAT = 1


def draw_shifts(key, part):
    count = 2 * LVL
    key_vals, key_order = jax.random.split(jax.random.fold_in(key, 5), 2)
    values = jax.random.randint(key_vals, (count,), 1, WIN)
    order = jax.random.permutation(key_order, count)
    values = values.at[order[0]].set(1)
    values = values.at[order[1]].set(WIN - 1)
    return values.reshape(LVL, 2).astype(jnp.int32)


def draw_bias_table(key, part):
    shape = (BANDS, NREL, HEADS)
    key_base = jax.random.fold_in(jax.random.fold_in(key, 11), 0)
    return jnp.clip(jax.random.normal(key_base, shape, jnp.float32), -4.0, 4.0)


def place_ends(drawn, stream_key, low, high):
    place = [jax.random.randint(jax.random.fold_in(stream_key, axis), (), 0, length) for axis, length in enumerate(drawn.shape)]
    widest = drawn.shape.index(max(drawn.shape))
    next_to = place[:widest] + [(place[widest] + 1) % drawn.shape[widest]] + place[widest + 1:]
    return drawn.at[tuple(place)].set(low).at[tuple(next_to)].set(high)


def block_levels(stream_key, extent, cuts, least, largest):
    level, own = 1.0, jax.random.fold_in(stream_key, 6)
    for dim, shards_of in cuts:
        draws = jnp.exp(jax.random.uniform(jax.random.fold_in(own, dim), (shards_of,), jnp.float32, least / len(cuts), largest / len(cuts)))
        level = level * jnp.repeat(draws, extent[dim] // shards_of).reshape([-1 if axis == dim else 1 for axis in range(len(extent))])
    return level


def normal_values(stream_key, shape, deviation, bound, cuts=(), held_as=jnp.bfloat16):
    entries = deviation * jax.random.normal(stream_key, shape, jnp.float32)
    if cuts:
        entries = entries * block_levels(stream_key, shape, cuts, -0.22, 0.18)
    return jnp.clip(entries, -bound, bound).astype(held_as)


def setup_inputs(seed: int = 0, part: int = 0) -> dict:
    key_list = jax.random.split(jax.random.key(seed), 10)
    part_splits = jax.random.split(jax.random.fold_in(key_list[9], part), 10)
    return {
        "tokens": normal_values(part_splits[0], (LVL, NLAT, NLON, D), 1.0, 6.0, ((2, 16),)),
        "land": place_ends((jax.random.randint(part_splits[1], (NLAT, NLON), 0, 10) < 3).astype(jnp.int32), jax.random.fold_in(part_splits[1], 1), 0, 1),
        "surface": normal_values(key_list[2], (2, D), 0.7, 4.0, (), jnp.float32),
        "gain": jnp.clip(1.0 + 0.15 * jax.random.normal(key_list[3], (D,), jnp.float32), 0.25, 1.75),
        "weights": normal_values(key_list[4], (D, 4 * HD), D ** -0.5, 0.15625, ((0, 16),)),
        "shifts": draw_shifts(jax.random.fold_in(key_list[9], 71), part),
        "index_table": place_ends(jax.random.randint(key_list[6], (WIN * WIN, WIN * WIN), 0, NREL), jax.random.fold_in(key_list[6], 1), 0, NREL - 1).astype(jnp.int32),
        "bias_table": draw_bias_table(jax.random.fold_in(key_list[9], 71), part),
        "cotangent": normal_values(part_splits[8], (LVL, NLAT, NLON, D), 1.0, 6.0, ((2, 16),)),
    }


epsilon = 1e-05

def rounded(values):
    return lax.optimization_barrier(values.astype(jnp.bfloat16)).astype(jnp.float32)

def normalize(stream, gain):
    values = stream.astype(jnp.float32)
    center = values - lax.optimization_barrier(jnp.mean(values, axis=-1, keepdims=True))
    spread = lax.rsqrt(lax.optimization_barrier(jnp.mean(center * center, axis=-1, keepdims=True)) + epsilon)
    return (center * spread * gain).astype(jnp.bfloat16)

def normalize_back(stream, gain, grad_normed):
    values = stream.astype(jnp.float32)
    center = values - lax.optimization_barrier(jnp.mean(values, axis=-1, keepdims=True))
    spread = lax.rsqrt(lax.optimization_barrier(jnp.mean(center * center, axis=-1, keepdims=True)) + epsilon)
    scaled = center * spread
    upstream = grad_normed.astype(jnp.float32) * gain
    return spread * (upstream - lax.optimization_barrier(jnp.mean(upstream, axis=-1, keepdims=True)) - scaled * lax.optimization_barrier(jnp.mean(upstream * scaled, axis=-1, keepdims=True)))

def roll_grid(field, shifts, sign):
    planes = []
    for level in range(field.shape[0]):
        planes.append(jnp.roll(field[level], (-sign * shifts[level, 0], -sign * shifts[level, 1]), axis=(0, 1)))
    return jnp.stack(planes)

def reference(tokens, land, surface, gain, weights, shifts, index_table, bias_table, cotangent):
    width = HEADS * HDIM
    area = WIN * WIN
    columns = NLON // WIN
    scale = 1.0 / math.sqrt(HDIM)
    surface_term = jnp.where(land[None, :, :, None] == 1, surface[1], surface[0])
    stream = (tokens.astype(jnp.float32) + surface_term).astype(jnp.bfloat16)
    normed = normalize(stream, gain)
    rolled = roll_grid(normed, shifts, 1)
    rolled_cot = roll_grid(cotangent, shifts, 1)
    w_qkv = weights[:, :3 * width]
    w_out = weights[:, 3 * width:]
    qkv = jnp.dot(rolled.reshape(-1, D), w_qkv, preferred_element_type=jnp.float32)
    view = rounded(qkv).reshape(LVL, N_LAT, WIN, columns, WIN, 3, HEADS, HDIM)
    query = view[:, :, :, :, :, 0]
    keys = view[:, :, :, :, :, 1]
    values = view[:, :, :, :, :, 2]
    six = (LVL, N_LAT, columns, HEADS, area, area)
    seven = (LVL, N_LAT, columns, HEADS, WIN, WIN, WIN, WIN)
    scores = jnp.einsum('liawbhd,licwehd->liwhabce', query, keys).reshape(six)
    onehot = (index_table[:, :, None] == jnp.arange(NREL, dtype=jnp.int32)).astype(jnp.float32)
    bias = jnp.einsum('qkr,srh->shqk', onehot, bias_table, precision=lax.Precision.HIGHEST)
    bias = bias.reshape(N_LAT, LVL, HEADS, area, area).transpose(1, 0, 2, 3, 4)
    rows = jnp.arange(NLAT, dtype=jnp.int32)
    group = rows[None, :] >= (NLAT - shifts[:, 0])[:, None]
    group = jnp.repeat(group.reshape(LVL, N_LAT, WIN), WIN, axis=2)
    allowed = group[:, :, :, None] == group[:, :, None, :]
    scores = scores * scale + bias[:, :, None]
    scores = jnp.where(allowed[:, :, None, None], scores, -1e+30)
    top = lax.optimization_barrier(jnp.max(scores, axis=-1, keepdims=True))
    expo = jnp.exp(scores - top)
    probs = expo / lax.optimization_barrier(jnp.sum(expo, axis=-1, keepdims=True))
    probs_b = rounded(probs).reshape(seven)
    mixed = jnp.einsum('liwhabce,licwehd->liawbhd', probs_b, values).astype(jnp.bfloat16)
    mixed_flat = mixed.reshape(-1, width)
    attended = jnp.dot(mixed_flat, w_out.T, preferred_element_type=jnp.float32).astype(jnp.bfloat16)
    attended = attended.reshape(LVL, NLAT, NLON, D)
    output = (stream.astype(jnp.float32) + roll_grid(attended, shifts, -1).astype(jnp.float32)).astype(jnp.bfloat16)
    cot_flat = rolled_cot.reshape(-1, D)
    grad_mixed = jnp.dot(cot_flat, w_out, preferred_element_type=jnp.float32)
    grad_mixed = rounded(grad_mixed).reshape(LVL, N_LAT, WIN, columns, WIN, HEADS, HDIM)
    grad_probs = jnp.einsum('liawbhd,licwehd->liwhabce', grad_mixed, values).reshape(six)
    grad_values = jnp.einsum('liwhabce,liawbhd->licwehd', probs_b, grad_mixed).astype(jnp.bfloat16)
    grad_scores = probs * (grad_probs - lax.optimization_barrier(jnp.sum(probs * grad_probs, axis=-1, keepdims=True)))
    grad_scores = rounded(grad_scores * scale).reshape(seven)
    grad_query = jnp.einsum('liwhabce,licwehd->liawbhd', grad_scores, keys).astype(jnp.bfloat16)
    grad_keys = jnp.einsum('liwhabce,liawbhd->licwehd', grad_scores, query).astype(jnp.bfloat16)
    grad_qkv = jnp.stack([grad_query, grad_keys, grad_values], axis=5).reshape(-1, 3 * width)
    grad_normed = jnp.dot(grad_qkv, w_qkv.T, preferred_element_type=jnp.float32).astype(jnp.bfloat16)
    grad_normed = roll_grid(grad_normed.reshape(LVL, NLAT, NLON, D), shifts, -1)
    grad_stream = normalize_back(stream, gain, grad_normed)
    grad_tokens = (cotangent.astype(jnp.float32) + grad_stream).astype(jnp.bfloat16)

    def split_tiles(field):
        return jnp.moveaxis(field.reshape(LVL, N_LAT, WIN, N_LON, CLON, -1), 3, 0)
    in_tiles = split_tiles(rolled)
    cot_tiles = split_tiles(rolled_cot)
    qkv_tiles = split_tiles(grad_qkv.reshape(LVL, NLAT, NLON, 3 * width))
    mixed_tiles = split_tiles(mixed_flat.reshape(LVL, NLAT, NLON, width))

    def add_tile(total, pieces):
        in_tile, cot_tile, qkv_tile, mixed_tile = pieces
        first = jnp.einsum('liacx,liacy->ixy', in_tile.astype(jnp.float32), qkv_tile.astype(jnp.float32))
        second = jnp.einsum('liacx,liacy->ixy', cot_tile.astype(jnp.float32), mixed_tile.astype(jnp.float32))
        part = rounded(jnp.concatenate([first, second], axis=2))
        return (total + lax.optimization_barrier(jnp.sum(part, axis=0)), None)
    total, _ = lax.scan(add_tile, jnp.zeros((D, 4 * width), jnp.float32), (in_tiles, cot_tiles, qkv_tiles, mixed_tiles))
    grad_weights = total * (1.0 / math.sqrt(LVL * NLAT * NLON))
    return (output, grad_tokens, grad_weights)
```

```python
import functools
import math

import jax
import jax.numpy as jnp
from jax import lax
from jax.experimental import pallas as pl
from jax.experimental.pallas import tpu as pltpu
from jax.sharding import PartitionSpec as P

epsilon = 1e-05
f32 = jnp.float32
bf16 = jnp.bfloat16
MESH = pl.DeviceIdType.MESH
VMEM = pl.BlockSpec(memory_space=pltpu.VMEM)
SMEM = pl.BlockSpec(memory_space=pltpu.SMEM)
MEMBERS = 4
CELLS = 128
MINE = 3


def passed_along(shard, axis, by):
    count = lax.axis_size(axis)
    return lax.ppermute(shard, axis, [(i, (i + by) % count) for i in range(count)])


def dot(a, b, dims):
    return lax.dot_general(a, b, ((dims[0], dims[1]), ((), ())), preferred_element_type=f32)


NN = ((1,), (0,))
NT = ((1,), (1,))
TN = ((0,), (0,))


def normalize(stream, gain):
    values = stream.astype(f32)
    center = values - jnp.mean(values, axis=-1, keepdims=True)
    spread = lax.rsqrt(jnp.mean(center * center, axis=-1, keepdims=True) + epsilon)
    return (center * spread * gain).astype(bf16)


def normalize_back(stream, gain, grad_normed):
    values = stream.astype(f32)
    center = values - jnp.mean(values, axis=-1, keepdims=True)
    spread = lax.rsqrt(jnp.mean(center * center, axis=-1, keepdims=True) + epsilon)
    scaled = center * spread
    upstream = grad_normed.astype(f32) * gain
    return spread * (
        upstream
        - jnp.mean(upstream, axis=-1, keepdims=True)
        - scaled * jnp.mean(upstream * scaled, axis=-1, keepdims=True)
    )


def take_rows(both, starts, length):
    taken = both[:, :, :length]
    for start in range(1, length + 1):
        here = (starts == start)[None, :, None, None, None]
        taken = jnp.where(here, both[:, :, start : start + length], taken)
    return taken


def layer_kernel(width, n, factor, w_own, fields, bias, shifts, back, out,
                 wown, W, X, XT, proj, G, U, edge, edge_in, gW, zbuf, F,
                 kept, core_out, core_in, y_out, y_in, roll_to, roll_from,
                 ws, wr, wzs, wzr, wxs, wxr, ts, tr, fs, fr, hs, hr, es, er,
                 zs_s, zs_r, gs_s, gs_r, cs, cr, ys, yr):
    me = lax.axis_index("lon")
    x = lax.axis_index("grp")
    z, m = me // 4, me % 4
    y, c = m // 2, m % 2
    last = n // 4 - 1
    depth = w_own.shape[0]
    model = depth * n
    plane = 4 * depth
    partner, across = 2 * y + 1 - c, 2 * (1 - y) + c
    diag = 3 - m
    up, down = (me + 4) % n, (me + n - 4) % n

    def remote(src, dst, ssem, rsem, lon):
        return pltpu.make_async_remote_copy(
            src, dst, ssem, rsem, device_id={"lon": lon}, device_id_type=MESH)

    barrier = pltpu.get_barrier_semaphore()
    for k in range(1, 4):
        pl.semaphore_signal(barrier, inc=1, device_id={"lon": 4 * z + (m + k) % 4}, device_id_type=MESH)
    for lon in (up, down):
        pl.semaphore_signal(barrier, inc=1, device_id={"lon": lon}, device_id_type=MESH)
    pl.semaphore_signal(barrier, inc=1, device_id={"grp": 1 - x}, device_id_type=MESH)

    left = lax.broadcasted_iota(jnp.int32, (CELLS, 128), 1) < 64
    left_d = lax.broadcasted_iota(jnp.int32, (depth, 128), 1) < 64

    for pair in range(2 * width // 256):
        for first in (0, 2):
            a = w_own[:, first * width + 128 * pair : first * width + 128 * pair + 128].astype(f32)
            b = w_own[:, (first + 1) * width + 128 * pair : (first + 1) * width + 128 * pair + 128].astype(f32)
            low = jnp.where(left_d, a, pltpu.roll(b, 64, 1)).astype(bf16)
            high = jnp.where(left_d, pltpu.roll(a, 64, 1), b).astype(bf16)
            for head, value in ((2 * pair, low), (2 * pair + 1, high)):
                wown[head // MINE, head % MINE, :, 64 * first : 64 * first + 128] = value
    for h in range(MINE):
        W[h, pl.ds(pl.multiple_of(me * depth, depth), depth), :] = wown[m, h]
    for f in range(2):
        X[f, m] = fields[f]

    pl.semaphore_wait(barrier, 6)

    def w_copy(h, k):
        to = (m + k) % 4
        rows = pl.ds(pl.multiple_of(me * depth, depth), depth)
        return remote(wown.at[to, h], W.at[h, rows], ws.at[h, k - 1], wr.at[h, k - 1], 4 * z + to)

    def token_copy(f, way):
        to = across if way == 0 else partner
        return remote(fields.at[f], X.at[f, m], ts.at[f, way], tr.at[f, way], 4 * z + to)

    def token_forward(f):
        return remote(X.at[f, across], X.at[f, across], fs.at[f], fr.at[f], 4 * z + partner)

    def two(zs, xx):
        return pl.ds(pl.multiple_of((4 * zs + 2 * xx) * depth, depth), 2 * depth)

    def wz_copy(h, zs, way):
        rows = two(zs, x)
        to = up if way == 0 else down
        return remote(W.at[h, rows], W.at[h, rows], wzs.at[h, zs, way], wzr.at[h, zs], to)

    def wx_copy(h, zs, xx):
        rows = two(zs, xx)
        return pltpu.make_async_remote_copy(
            W.at[h, rows], W.at[h, rows], wxs.at[h, zs], wxr.at[h, zs],
            device_id={"grp": 1 - x}, device_id_type=MESH)

    for h in range(MINE):
        for k in (2, 1, 3):
            w_copy(h, k).start()
    for f in range(2):
        for way in range(2):
            token_copy(f, way).start()

    lane = lax.broadcasted_iota(jnp.int32, (CELLS, 2 * CELLS), 1)
    cell = lax.broadcasted_iota(jnp.int32, (CELLS, 2 * CELLS), 0)

    def source(window_cell):
        lev, row, col = window_cell >> 6, (window_cell >> 3) & 7, window_cell & 7
        from_row = (row + jnp.where(lev == 0, shifts[0, 0], shifts[1, 0])) & 7
        from_col = col + jnp.where(lev == 0, shifts[0, 1], shifts[1, 1])
        return lev * 64 + from_row * 8 + (from_col & 7), from_col >= 8

    src, east = source(cell)
    roll_to[...] = jnp.where(src + jnp.where(east, CELLS, 0) == lane, 1.0, 0.0).astype(bf16)
    src, east = source(lane & 127)
    hit = (src == cell) & (jnp.where(east, 1, 0) == jnp.where(lane < CELLS, 1, 0))
    roll_from[...] = jnp.where(hit, 1.0, 0.0).astype(bf16)

    def spread(h, zs, act, to_up, to_down):
        if to_up:
            pl.when(z < last)(lambda: act(wz_copy(h, zs, 0)))
        if to_down:
            pl.when(z > 0)(lambda: act(wz_copy(h, zs, 1)))

    start = lambda copy: copy.start()
    sent = lambda copy: copy.wait_send()
    for h in range(MINE):
        for k in (2, 1, 3):
            w_copy(h, k).wait_recv()
        spread(h, z, start, True, True)

    def transpose(t):
        for f in range(2):
            def chunk(i, _):
                cols = pl.ds(pl.multiple_of(i * 512, 512), 512)
                XT[f, cols, pl.ds(pl.multiple_of(t * CELLS, CELLS), CELLS)] = (
                    X[f, t, :, cols].astype(f32).T.astype(bf16))
                return 0
            lax.fori_loop(0, model // 512, chunk, 0)

    def from_planes(t, act):
        pl.when(z - t >= 0)(lambda: act(z - t, dict(to_up=True, to_down=False)))
        pl.when(z + t <= last)(lambda: act(z + t, dict(to_up=False, to_down=True)))

    def weights_arrived(zs, ways):
        for h in range(MINE):
            wz_copy(h, zs, 0).wait_recv()
            spread(h, zs, start, **ways)
            wx_copy(h, zs, x).start()

    transpose(m)
    from_planes(1, weights_arrived)
    for f in range(2):
        token_copy(f, 1).wait_recv()
    transpose(partner)
    from_planes(2, weights_arrived)
    from_planes(3, weights_arrived)
    for f in range(2):
        token_copy(f, 0).wait_recv()
        token_forward(f).start()
    transpose(across)
    for f in range(2):
        token_forward(f).wait_recv()
    transpose(diag)

    def halo_copy(h):
        return remote(proj.at[h, 0], proj.at[h, MEMBERS], hs.at[h], hr.at[h], down)

    left_all = lax.broadcasted_iota(jnp.int32, (MEMBERS * CELLS, 128), 1) < 64
    for h in range(MINE):
        def wait_x(zs, ways):
            wx_copy(h, zs, 1 - x).wait_recv()
        for t in range(1, last + 1):
            from_planes(t, wait_x)
        normed = dot(X[0].reshape(MEMBERS * CELLS, model), W[h], NN)
        grads = dot(X[1].reshape(MEMBERS * CELLS, model), W[h, :, 128:], NN)
        high = jnp.where(left_all, normed[:, 128:], grads)
        proj[h, :MEMBERS, :, :128] = normed[:, :128].astype(bf16).reshape(MEMBERS, CELLS, 128)
        proj[h, :MEMBERS, :, 128:] = high.astype(bf16).reshape(MEMBERS, CELLS, 128)
        halo_copy(h).start()

    def window(h, w):
        rolled = dot(roll_to[...], proj[h, w : w + 2].reshape(2 * CELLS, 256), NN)
        qk, vg = rolled[:, :128], rolled[:, 128:]
        kq, gv = pltpu.roll(qk, 64, 1).astype(bf16), pltpu.roll(vg, 64, 1).astype(bf16)
        q = jnp.where(left, qk, 0.0).astype(bf16)
        g = jnp.where(left, gv.astype(f32), 0.0).astype(bf16)
        s = dot(q, kq, NT) * 0.125 + bias[h]
        top = jnp.max(s, axis=-1, keepdims=True)
        expo = jnp.exp(s - top)
        probs = expo / jnp.sum(expo, axis=-1, keepdims=True)
        probs_b = probs.astype(bf16)
        grad_probs = dot(g, vg.astype(bf16), NT)
        inner = jnp.sum(probs * grad_probs, axis=-1, keepdims=True)
        gs = (probs * (grad_probs - inner) * 0.125).astype(bf16)
        G[h, w, :, :128] = jnp.where(left, dot(gs, kq, NN), dot(gs, kq, TN)).astype(bf16)
        G[h, w, :, 128:] = jnp.where(left, dot(probs_b, gv, TN), dot(probs_b, gv, NN)).astype(bf16)

    def edge_copy(h):
        return remote(edge.at[h], edge_in.at[h], es.at[h], er.at[h], up)

    def attend(h):
        for w in range(MEMBERS - 1):
            window(h, w)
        halo_copy(h).wait_recv()
        window(h, MEMBERS - 1)
        edge[h] = dot(roll_from[:, :CELLS], G[h, MEMBERS - 1], NN).astype(bf16)
        edge_copy(h).start()
        for t in range(1, MEMBERS):
            U[h, t] = dot(roll_from[...], G[h, t - 1 : t + 1].reshape(2 * CELLS, 256), NN).astype(bf16)

    order = [3 - 3 * (z // 2), (2 + 3 * z) % 5, 1 + z % 2, z]

    def weight_grads(h):
        edge_copy(h).wait_recv()
        own = dot(roll_from[:, CELLS:], G[h, 0], NN)
        U[h, 0] = (own + edge_in[h].astype(f32)).astype(bf16)
        all_cells = U[h].reshape(MEMBERS * CELLS, 256)
        left_p = lax.broadcasted_iota(jnp.int32, (plane, 128), 1) < 64
        for d in order:
            rows = pl.ds(pl.multiple_of(d * plane, plane), plane)
            first = dot(XT[0, rows, :], all_cells, NN)
            second = dot(XT[1, rows, :], all_cells[:, 128:], NN)
            gW[h, d, :, :128] = first[:, :128].astype(bf16)
            gW[h, d, :, 128:] = jnp.where(left_p, first[:, 128:], second).astype(bf16)

    def z_copy(h, d, way):
        return remote(gW.at[h, d], zbuf.at[h, d, way], zs_s.at[h, d], zs_r.at[h, d, way],
                      up if way == 0 else down)

    def add(h, d, *ways):
        total = gW[h, d].astype(f32)
        for way in ways:
            total += zbuf[h, d, way].astype(f32)
        gW[h, d] = total.astype(bf16)

    def final_copy(h, k):
        to = (m + k) % 4
        rows = pl.ds(pl.multiple_of(to * depth, depth), depth)
        return remote(gW.at[h, z, rows], F.at[h, m], gs_s.at[h, k - 1], gs_r.at[h, k - 1], 4 * z + to)

    def line_step(h, i):
        d = order[i]

        def go_up():
            def more():
                z_copy(h, d, 0).wait_recv()
                add(h, d, 0)
            pl.when(z > 0)(more)
            z_copy(h, d, 0).start()

        def go_down():
            def more():
                z_copy(h, d, 1).wait_recv()
                add(h, d, 1)
            pl.when(z < last)(more)
            z_copy(h, d, 1).start()

        if i < last:
            pl.when(d > z)(go_up)
            pl.when(d < z)(go_down)
            return

        def from_below():
            z_copy(h, d, 0).wait_recv()
            add(h, d, 0)

        def from_above():
            z_copy(h, d, 1).wait_recv()
            add(h, d, 1)
        pl.when(z > 0)(from_below)
        pl.when(z < last)(from_above)
        for k in (2, 1, 3):
            final_copy(h, k).start()
        F[h, m] = gW[h, z, pl.ds(pl.multiple_of(m * depth, depth), depth), :]

    def results(core, put):
        left_two = lax.broadcasted_iota(jnp.int32, (2 * CELLS, 128), 1) < 64

        def chunk(i, _):
            cols = pl.ds(pl.multiple_of(i * 512, 512), 512)
            attended = jnp.zeros((2 * CELLS, 512), f32)
            normed = jnp.zeros((2 * CELLS, 512), f32)
            for h in range(MINE):
                cells = jnp.concatenate([U[h, core], U[h, 2 + core]], axis=0)
                zero = jnp.zeros((2 * CELLS, 128), bf16)
                low, high = cells[:, :128], cells[:, 128:]
                attended += dot(jnp.where(left_two, zero, high), W[h, cols, 128:], NT)
                values = jnp.concatenate([low, jnp.where(left_two, high, zero)], axis=1)
                normed += dot(values, W[h, cols, :], NT)
            put(cols, (attended, normed))
            return 0
        lax.fori_loop(0, model // 512, chunk, 0)

    def core_copy():
        return remote(core_out, core_in, cs, cr, 4 * z + partner)

    def y_copy():
        return remote(y_out, y_in, ys, yr, 4 * z + across)

    def put_out(cols, both):
        for f in range(2):
            for yy in range(2):
                core_out[f, yy, :, cols] = both[f][yy * CELLS : (yy + 1) * CELLS].astype(bf16)

    def put_kept(cols, both):
        for f in range(2):
            for yy in range(2):
                kept[f, yy, :, cols] = both[f][yy * CELLS : (yy + 1) * CELLS]

    for h in range(MINE):
        attend(h)
        if h > 0:
            weight_grads(h - 1)
            line_step(h - 1, 0)
    weight_grads(MINE - 1)
    line_step(MINE - 1, 0)
    line_step(0, 1)
    results(1 - c, put_out)
    core_copy().start()
    line_step(1, 1)
    line_step(0, 2)
    results(c, put_kept)
    core_copy().wait_recv()
    for f in range(2):
        y_out[f] = (kept[f, 1 - y] + core_in[f, 1 - y].astype(f32)).astype(bf16)
    y_copy().start()
    line_step(2, 1)
    line_step(1, 2)
    line_step(0, 3)
    line_step(2, 2)
    line_step(1, 3)
    y_copy().wait_recv()
    for f in range(2):
        back[f] = (kept[f, y] + core_in[f, y].astype(f32) + y_in[f].astype(f32)).astype(bf16)
    line_step(2, 3)

    for h in range(MINE):
        for k in (2, 1, 3):
            final_copy(h, k).wait_recv()
    for pair in range(2 * width // 256):
        for first in (0, 2):
            low, high = (
                F[head % MINE, head // MINE, :, 64 * first : 64 * first + 128].astype(f32) * factor
                for head in (2 * pair, 2 * pair + 1))
            a = jnp.where(left_d, low, pltpu.roll(high, 64, 1))
            b = jnp.where(left_d, pltpu.roll(low, 64, 1), high)
            out[:, first * width + 128 * pair : first * width + 128 * pair + 128] = a
            out[:, (first + 1) * width + 128 * pair : (first + 1) * width + 128 * pair + 128] = b

    for h in range(MINE):
        for k in (2, 1, 3):
            w_copy(h, k).wait_send()
            final_copy(h, k).wait_send()
        spread(h, z, sent, True, True)
        halo_copy(h).wait_send()
        edge_copy(h).wait_send()
        for i in range(last):
            z_copy(h, order[i], 0).wait_send()

    def weights_sent(zs, ways):
        for h in range(MINE):
            spread(h, zs, sent, **ways)
            wx_copy(h, zs, x).wait_send()

    for t in range(1, last + 1):
        from_planes(t, weights_sent)
    for f in range(2):
        for way in range(2):
            token_copy(f, way).wait_send()
        token_forward(f).wait_send()
    core_copy().wait_send()
    y_copy().wait_send()


def on_device(tokens, land, surface, gain, weights, shifts, index_table, bias_table, cotangent):
    levels, tile_rows, tile_cols, model = tokens.shape
    entries = bias_table.shape[1]
    width = weights.shape[1] // 4
    count = levels * tile_rows * tile_cols
    area = tile_rows * tile_rows
    lats = lax.axis_size("lat")
    n = lax.axis_size("lon")
    depth = model // n
    dma = pltpu.SemaphoreType.DMA

    surface_term = jnp.where(land[None, :, :, None] == 1, surface[1], surface[0])
    stream = (tokens.astype(f32) + surface_term).astype(bf16)
    fields = jnp.stack([normalize(stream, gain), cotangent])
    tile_shifts = shifts
    if lats > 1:
        below = passed_along(fields, "lat", -1)
        both = jnp.concatenate([fields, below], axis=2)
        fields = take_rows(both, shifts[:, 0], tile_rows)
        tile_shifts = shifts * jnp.array([[0, 1]], jnp.int32)
    mine = fields.reshape(2, count, model)

    table = lax.dynamic_slice_in_dim(bias_table, MINE * (lax.axis_index("lon") % MEMBERS), MINE, 2)
    onehot = (index_table[:, :, None] == jnp.arange(entries, dtype=jnp.int32)).astype(f32)
    bias = jnp.einsum("qkr,lrh->hlqk", onehot, table, precision=lax.Precision.HIGHEST)
    total_rows = tile_rows * lats
    row_number = lax.axis_index("lat") * tile_rows + jnp.arange(tile_rows, dtype=jnp.int32)
    group = row_number[None, :] >= (total_rows - shifts[:, 0])[:, None]
    group = jnp.repeat(group, tile_rows, axis=1)
    allowed = group[:, :, None] == group[:, None, :]
    bias = jnp.where(allowed[None], bias, -1e30)
    other = jnp.full((MINE, area, area), -jnp.inf, f32)
    bias = jnp.concatenate(
        [jnp.concatenate([bias[:, 0], other], axis=2), jnp.concatenate([other, bias[:, 1]], axis=2)],
        axis=1,
    )

    factor = 1.0 / math.sqrt(count * lats * n)
    plane = MEMBERS * depth
    last = n // MEMBERS
    vm = pltpu.VMEM
    back, grad_weights = pl.pallas_call(
        functools.partial(layer_kernel, width, n, factor),
        name="layer",
        out_shape=(
            jax.ShapeDtypeStruct((2, count, model), bf16),
            jax.ShapeDtypeStruct((depth, 4 * width), f32),
        ),
        in_specs=[VMEM, VMEM, VMEM, SMEM],
        out_specs=(VMEM, VMEM),
        scratch_shapes=[
            vm((MEMBERS, MINE, depth, 256), bf16),
            vm((MINE, model, 256), bf16),
            vm((2, MEMBERS, count, model), bf16),
            vm((2, model, MEMBERS * count), bf16),
            vm((MINE, MEMBERS + 1, count, 256), bf16),
            vm((MINE, MEMBERS, count, 256), bf16),
            vm((MINE, MEMBERS, count, 256), bf16),
            vm((MINE, count, 256), bf16),
            vm((MINE, count, 256), bf16),
            vm((MINE, last, plane, 256), bf16),
            vm((MINE, last, 2, plane, 256), bf16),
            vm((MINE, MEMBERS, depth, 256), bf16),
            vm((2, 2, count, model), f32),
            vm((2, 2, count, model), bf16),
            vm((2, 2, count, model), bf16),
            vm((2, count, model), bf16),
            vm((2, count, model), bf16),
            vm((count, 2 * count), bf16),
            vm((count, 2 * count), bf16),
            dma((MINE, 3)), dma((MINE, 3)),
            dma((MINE, last, 2)), dma((MINE, last)),
            dma((MINE, last)), dma((MINE, last)),
            dma((2, 2)), dma((2, 2)), dma((2,)), dma((2,)),
            dma((MINE,)), dma((MINE,)), dma((MINE,)), dma((MINE,)),
            dma((MINE, last)), dma((MINE, last, 2)),
            dma((MINE, 3)), dma((MINE, 3)),
            dma, dma, dma, dma,
        ],
        compiler_params=pltpu.CompilerParams(
            collective_id=0, has_side_effects=True, vmem_limit_bytes=60 * 2**20
        ),
        cost_estimate=pl.CostEstimate(flops=8 * 10**9, bytes_accessed=10 * 10**6, transcendentals=200000),
    )(weights, mine, bias, tile_shifts)
    back = back.reshape(2, levels, tile_rows, tile_cols, model)
    if lats > 1:
        above = passed_along(back, "lat", 1)
        both = jnp.concatenate([above, back], axis=2)
        back = take_rows(both, tile_rows - shifts[:, 0], tile_rows)
    output = (stream.astype(f32) + back[0].astype(f32)).astype(bf16)
    grad_stream = normalize_back(stream, gain, back[1])
    grad_tokens = (cotangent.astype(f32) + grad_stream).astype(bf16)
    if lats > 1:
        grad_weights = lax.psum(grad_weights, "lat")
    return (output, grad_tokens, grad_weights)


def solution(mesh):
    return jax.shard_map(
        on_device,
        mesh=mesh,
        in_specs=(
            P("grp", "lat", "lon", None),
            P(("grp", "lat"), "lon"),
            P(),
            P(),
            P("lon", None),
            P(),
            P(),
            P("lat", None, None),
            P("grp", "lat", "lon", None),
        ),
        out_specs=(
            P("grp", "lat", "lon", None),
            P("grp", "lat", "lon", None),
            P(("grp", "lon"), None),
        ),
        check_vma=False,
    )
```

```python
import functools
import math

import jax
import jax.numpy as jnp
from jax import lax
from jax.experimental import pallas as pl
from jax.experimental.pallas import tpu as pltpu
from jax.sharding import PartitionSpec as P

epsilon = 1e-05
f32 = jnp.float32
bf16 = jnp.bfloat16
MESH = pl.DeviceIdType.MESH
VMEM = pl.BlockSpec(memory_space=pltpu.VMEM)
SMEM = pl.BlockSpec(memory_space=pltpu.SMEM)
MEMBERS = 4
CELLS = 128
MINE = 3


def passed_along(shard, axis, by):
    count = lax.axis_size(axis)
    return lax.ppermute(shard, axis, [(i, (i + by) % count) for i in range(count)])


def dot(a, b, dims):
    return lax.dot_general(a, b, ((dims[0], dims[1]), ((), ())), preferred_element_type=f32)


NN = ((1,), (0,))
NT = ((1,), (1,))
TN = ((0,), (0,))


def normalize(stream, gain):
    values = stream.astype(f32)
    center = values - jnp.mean(values, axis=-1, keepdims=True)
    spread = lax.rsqrt(jnp.mean(center * center, axis=-1, keepdims=True) + epsilon)
    return (center * spread * gain).astype(bf16)


def normalize_back(stream, gain, grad_normed):
    values = stream.astype(f32)
    center = values - jnp.mean(values, axis=-1, keepdims=True)
    spread = lax.rsqrt(jnp.mean(center * center, axis=-1, keepdims=True) + epsilon)
    scaled = center * spread
    upstream = grad_normed.astype(f32) * gain
    return spread * (
        upstream
        - jnp.mean(upstream, axis=-1, keepdims=True)
        - scaled * jnp.mean(upstream * scaled, axis=-1, keepdims=True)
    )


def take_rows(both, starts, length):
    taken = both[:, :, :length]
    for start in range(1, length + 1):
        here = (starts == start)[None, :, None, None, None]
        taken = jnp.where(here, both[:, :, start : start + length], taken)
    return taken


def layer_kernel(width, n, lats, factor, *refs):
    if lats > 1:
        w_own, fields, table, index, shifts, *refs = refs
        outs, refs = refs[:2], refs[2:]
    else:
        w_own, tokens, cot, land, surface, gain, table, index, shifts, *refs = refs
        outs, refs = refs[:3], refs[3:]
    (bias, stream,
                 wown, W, X, XT, proj, G, U, edge, edge_in, gW, zbuf, F,
                 kept, core_out, core_in, y_out, y_in, roll_to, roll_from,
                 wps, wpr, wys, wyr, wzs, wzr, wxs, wxr, ts, tr, fs, fr, hs, hr, es, er,
                 zs_s, zs_r, gs_s, gs_r, cs, cr, ys, yr) = refs
    out = outs[-1]
    me = lax.axis_index("lon")
    x = lax.axis_index("grp")
    z, m = me // 4, me % 4
    y, c = m // 2, m % 2
    last = n // 4 - 1
    depth = w_own.shape[0]
    model = depth * n
    plane = 4 * depth
    partner, across = 2 * y + 1 - c, 2 * (1 - y) + c
    diag = 3 - m
    up, down = (me + 4) % n, (me + n - 4) % n

    def remote(src, dst, ssem, rsem, lon):
        return pltpu.make_async_remote_copy(
            src, dst, ssem, rsem, device_id={"lon": lon}, device_id_type=MESH)

    barrier = pltpu.get_barrier_semaphore()
    for k in range(1, 4):
        pl.semaphore_signal(barrier, inc=1, device_id={"lon": 4 * z + (m + k) % 4}, device_id_type=MESH)
    for lon in (up, down):
        pl.semaphore_signal(barrier, inc=1, device_id={"lon": lon}, device_id_type=MESH)
    pl.semaphore_signal(barrier, inc=1, device_id={"grp": 1 - x}, device_id_type=MESH)

    left = lax.broadcasted_iota(jnp.int32, (CELLS, 128), 1) < 64
    left_d = lax.broadcasted_iota(jnp.int32, (depth, 128), 1) < 64

    for pair in range(2 * width // 256):
        for first in (0, 2):
            a = w_own[:, first * width + 128 * pair : first * width + 128 * pair + 128].astype(f32)
            b = w_own[:, (first + 1) * width + 128 * pair : (first + 1) * width + 128 * pair + 128].astype(f32)
            low = jnp.where(left_d, a, pltpu.roll(b, 64, 1)).astype(bf16)
            high = jnp.where(left_d, pltpu.roll(a, 64, 1), b).astype(bf16)
            for head, value in ((2 * pair, low), (2 * pair + 1, high)):
                wown[head // MINE, head % MINE, :, 64 * first : 64 * first + 128] = value
    for h in range(MINE):
        W[h, z, y, c] = wown[m, h]
    if lats > 1:
        for f in range(2):
            X[f, m] = fields[f]
    else:
        X[1, m] = cot[...]

    pl.semaphore_wait(barrier, 6)

    def wp_copy(h):
        return remote(wown.at[partner, h], W.at[h, z, y, c], wps.at[h], wpr.at[h], 4 * z + partner)

    def wy_copy(h, core):
        to = 2 * (1 - y) + core
        return remote(wown.at[to, h], W.at[h, z, y, c], wys.at[h, core], wyr.at[h], 4 * z + to)

    def token_copy(f, way):
        to = across if way == 0 else partner
        return remote(X.at[f, m], X.at[f, m], ts.at[f, way], tr.at[f, way], 4 * z + to)

    def token_forward(f):
        return remote(X.at[f, across], X.at[f, across], fs.at[f], fr.at[f], 4 * z + partner)

    def wz_copy(h, zs, way):
        block = W.at[h, zs, :, x]
        to = up if way == 0 else down
        return remote(block, block, wzs.at[h, zs, way], wzr.at[h, zs], to)

    def wx_copy(h, zs, xx, here=False):
        block = W.at[h, zs, 1 - y, xx] if here else W.at[h, zs, :, xx]
        return pltpu.make_async_remote_copy(
            block, block, wxs.at[h, zs], wxr.at[h, zs], device_id={"grp": 1 - x}, device_id_type=MESH)

    def wy_all(h, act):
        def both():
            for core in range(2):
                act(wy_copy(h, core))
        pl.when(c == x)(both)

    start = lambda copy: copy.start()
    sent = lambda copy: copy.wait_send()
    for h in range(MINE):
        wp_copy(h).start()
        wy_all(h, start)
    for way in range(2):
        token_copy(1, way).start()
    if lats == 1:
        place = lax.broadcasted_iota(jnp.int32, (CELLS, 8), 0)
        spot = lax.broadcasted_iota(jnp.int32, (CELLS, 8), 1)
        row_hit = jnp.where(((place >> 3) & 7) == spot, 1.0, 0.0)
        marks = jnp.where((place & 7) == spot, dot(row_hit, land[...].astype(f32), NN), 0.0)
        on_land = jnp.sum(marks, axis=-1, keepdims=True) > 0.5
        term = jnp.where(on_land, surface[1:2, :], surface[0:1, :])
        stream[...] = (tokens[...].astype(f32) + term).astype(bf16)
        X[0, m] = normalize(stream[...], gain[...])
    for way in range(2):
        token_copy(0, way).start()

    lane = lax.broadcasted_iota(jnp.int32, (CELLS, 2 * CELLS), 1)
    cell = lax.broadcasted_iota(jnp.int32, (CELLS, 2 * CELLS), 0)

    def source(window_cell):
        lev, row, col = window_cell >> 6, (window_cell >> 3) & 7, window_cell & 7
        from_row = row
        if lats == 1:
            from_row = (row + jnp.where(lev == 0, shifts[0, 0], shifts[1, 0])) & 7
        from_col = col + jnp.where(lev == 0, shifts[0, 1], shifts[1, 1])
        return lev * 64 + from_row * 8 + (from_col & 7), from_col >= 8

    src, east = source(cell)
    roll_to[...] = jnp.where(src + jnp.where(east, CELLS, 0) == lane, 1.0, 0.0).astype(bf16)
    src, east = source(lane & 127)
    hit = (src == cell) & (jnp.where(east, 1, 0) == jnp.where(lane < CELLS, 1, 0))
    roll_from[...] = jnp.where(hit, 1.0, 0.0).astype(bf16)

    def spread(h, zs, act, to_up, to_down):
        if to_up:
            pl.when(z < last)(lambda: act(wz_copy(h, zs, 0)))
        if to_down:
            pl.when(z > 0)(lambda: act(wz_copy(h, zs, 1)))


    def transpose(t):
        for f in range(2):
            def chunk(i, _):
                cols = pl.ds(pl.multiple_of(i * 512, 512), 512)
                XT[f, cols, pl.ds(pl.multiple_of(t * CELLS, CELLS), CELLS)] = (
                    X[f, t, :, cols].astype(f32).T.astype(bf16))
                return 0
            lax.fori_loop(0, model // 512, chunk, 0)

    def from_planes(t, act):
        pl.when(z - t >= 0)(lambda: act(z - t, dict(to_up=True, to_down=False)))
        pl.when(z + t <= last)(lambda: act(z + t, dict(to_up=False, to_down=True)))

    def make_bias():
        area = CELLS // 2
        half = lax.broadcasted_iota(jnp.int32, (area, CELLS), 1) < area
        entry = jnp.concatenate([index[...], index[...]], axis=1)
        unroll = next(u for u in (5, 3, 1) if table.shape[1] % u == 0)

        def some(i, found):
            for u in range(unroll):
                r = i * unroll + u
                here = entry == r
                found = tuple(
                    jnp.where(here, jnp.where(half, table[0, r, MINE * m + h], table[1, r, MINE * m + h]), found[h])
                    for h in range(MINE))
            return found

        found = lax.fori_loop(
            0, table.shape[1] // unroll, some, tuple(jnp.zeros((area, CELLS), f32) for _ in range(MINE)))
        query = lax.broadcasted_iota(jnp.int32, (area, CELLS), 0) >> 3
        key = (lax.broadcasted_iota(jnp.int32, (area, CELLS), 1) & 63) >> 3
        first_row = 0 if lats == 1 else 8 * lax.axis_index("lat")
        for lev in range(2):
            edge_row = 8 * lats - shifts[lev, 0] - first_row
            same = jnp.where(query >= edge_row, 1, 0) == jnp.where(key >= edge_row, 1, 0)
            keep = half if lev == 0 else jnp.logical_not(half)
            for h in range(MINE):
                masked = jnp.where(same, found[h], -1e30)
                bias[h, lev * area : (lev + 1) * area, :] = jnp.where(keep, masked, -jnp.inf)

    def weights_arrived(t, h):
        if t == 0:
            wp_copy(h).wait_recv()
            wy_copy(h, 0).wait_recv()
            spread(h, z, start, True, True)
            wx_copy(h, z, x, True).start()
            return

        def arrived(zs, ways):
            wz_copy(h, zs, 0).wait_recv()
            spread(h, zs, start, **ways)
            wx_copy(h, zs, x).start()
        from_planes(t, arrived)

    def tokens_across(f):
        token_copy(f, 0).wait_recv()
        token_forward(f).start()

    weights_arrived(0, 0)
    weights_arrived(1, 0)
    weights_arrived(0, 1)
    transpose(m)
    weights_arrived(2, 0)
    weights_arrived(1, 1)
    weights_arrived(0, 2)
    make_bias()
    for f in range(2):
        token_copy(f, 1).wait_recv()
    transpose(partner)
    weights_arrived(3, 0)
    tokens_across(1)
    weights_arrived(2, 1)
    weights_arrived(1, 2)
    weights_arrived(3, 1)
    tokens_across(0)
    weights_arrived(2, 2)
    transpose(across)
    for f in range(2):
        token_forward(f).wait_recv()
    transpose(diag)

    def halo_copy(h):
        return remote(proj.at[h, 0], proj.at[h, MEMBERS], hs.at[h], hr.at[h], down)

    left_all = lax.broadcasted_iota(jnp.int32, (MEMBERS * CELLS, 128), 1) < 64

    def project(h):
        def wait_x(zs, ways):
            wx_copy(h, zs, 1 - x).wait_recv()
        wx_copy(h, z, 1 - x, True).wait_recv()
        for t in range(1, last + 1):
            from_planes(t, wait_x)
        w = W[h].reshape(model, 256)
        normed = dot(X[0].reshape(MEMBERS * CELLS, model), w, NN)
        grads = dot(X[1].reshape(MEMBERS * CELLS, model), w[:, 128:], NN)
        high = jnp.where(left_all, normed[:, 128:], grads)
        proj[h, :MEMBERS, :, :128] = normed[:, :128].astype(bf16).reshape(MEMBERS, CELLS, 128)
        proj[h, :MEMBERS, :, 128:] = high.astype(bf16).reshape(MEMBERS, CELLS, 128)
        halo_copy(h).start()

    def windows(h, which):
        each = range(len(which))
        zero = jnp.zeros((CELLS, 128), bf16)
        rolled = [dot(roll_to[...], proj[h, w : w + 2].reshape(2 * CELLS, 256), NN) for w in which]
        swapped = [(pltpu.roll(r[:, :128], 64, 1).astype(bf16), pltpu.roll(r[:, 128:], 64, 1).astype(bf16)) for r in rolled]
        q = [jnp.where(left, r[:, :128].astype(bf16), zero) for r in rolled]
        g = [jnp.where(left, gv, zero) for _, gv in swapped]
        s = [dot(q[i], swapped[i][0], NT) * 0.125 + bias[h] for i in each]
        grad_probs = [dot(g[i], rolled[i][:, 128:].astype(bf16), NT) for i in each]
        top = [jnp.max(a, axis=-1, keepdims=True) for a in s]
        expo = [jnp.exp(s[i] - top[i]) for i in each]
        total = [jnp.sum(a, axis=-1, keepdims=True) for a in expo]
        probs = [expo[i] / total[i] for i in each]
        probs_b = [a.astype(bf16) for a in probs]
        inner = [jnp.sum(probs[i] * grad_probs[i], axis=-1, keepdims=True) for i in each]
        gs = [(probs[i] * (grad_probs[i] - inner[i]) * 0.125).astype(bf16) for i in each]
        for i in each:
            kq, gv = swapped[i]
            G[h, which[i], :, 128:] = jnp.where(left, dot(probs_b[i], gv, TN), dot(probs_b[i], gv, NN)).astype(bf16)
            G[h, which[i], :, :128] = jnp.where(left, dot(gs[i], kq, NN), dot(gs[i], kq, TN)).astype(bf16)

    def edge_copy(h):
        return remote(edge.at[h], edge_in.at[h], es.at[h], er.at[h], up)

    def attend(h):
        halo_copy(h).wait_recv()
        windows(h, list(range(MEMBERS)))
        edge[h] = dot(roll_from[:, :CELLS], G[h, MEMBERS - 1], NN).astype(bf16)
        edge_copy(h).start()
        for t in range(1, MEMBERS):
            U[h, t] = dot(roll_from[...], G[h, t - 1 : t + 1].reshape(2 * CELLS, 256), NN).astype(bf16)

    order = [3 - 3 * (z // 2), (2 + 3 * z) % 5, 1 + z % 2, z]

    def weight_grads(h):
        edge_copy(h).wait_recv()
        own = dot(roll_from[:, CELLS:], G[h, 0], NN)
        U[h, 0] = (own + edge_in[h].astype(f32)).astype(bf16)
        all_cells = U[h].reshape(MEMBERS * CELLS, 256)
        left_p = lax.broadcasted_iota(jnp.int32, (plane, 128), 1) < 64
        for d in order:
            rows = pl.ds(pl.multiple_of(d * plane, plane), plane)
            first = dot(XT[0, rows, :], all_cells, NN)
            second = dot(XT[1, rows, :], all_cells[:, 128:], NN)
            gW[h, d, :, :128] = first[:, :128].astype(bf16)
            gW[h, d, :, 128:] = jnp.where(left_p, first[:, 128:], second).astype(bf16)

            def send_up():
                z_copy(h, d, 0).start()

            def send_down():
                z_copy(h, d, 1).start()
            pl.when((z == 0) & (d != z))(send_up)
            pl.when((z == last) & (d != z))(send_down)

    def z_copy(h, d, way):
        return remote(gW.at[h, d], zbuf.at[h, d, way], zs_s.at[h, d], zs_r.at[h, d, way],
                      up if way == 0 else down)

    def add(h, d, *ways):
        total = gW[h, d].astype(f32)
        for way in ways:
            total += zbuf[h, d, way].astype(f32)
        gW[h, d] = total.astype(bf16)

    def final_copy(h, k):
        to = (m + k) % 4
        rows = pl.ds(pl.multiple_of(to * depth, depth), depth)
        return remote(gW.at[h, z, rows], F.at[h, m], gs_s.at[h, k - 1], gs_r.at[h, k - 1], 4 * z + to)

    def line_step(h, i):
        d = order[i]

        def go_up():
            z_copy(h, d, 0).wait_recv()
            add(h, d, 0)
            z_copy(h, d, 0).start()

        def go_down():
            z_copy(h, d, 1).wait_recv()
            add(h, d, 1)
            z_copy(h, d, 1).start()

        if i < last:
            pl.when((d > z) & (z > 0))(go_up)
            pl.when((d < z) & (z < last))(go_down)
            return

        def from_below():
            z_copy(h, d, 0).wait_recv()
            add(h, d, 0)

        def from_above():
            z_copy(h, d, 1).wait_recv()
            add(h, d, 1)
        pl.when(z > 0)(from_below)
        pl.when(z < last)(from_above)
        for k in (2, 1, 3):
            final_copy(h, k).start()
        F[h, m] = gW[h, z, pl.ds(pl.multiple_of(m * depth, depth), depth), :]

    def results(core, put):
        left_two = lax.broadcasted_iota(jnp.int32, (2 * CELLS, 128), 1) < 64

        def chunk(i, _):
            cols = pl.ds(pl.multiple_of(i * plane, plane), plane)
            attended = jnp.zeros((2 * CELLS, plane), f32)
            normed = jnp.zeros((2 * CELLS, plane), f32)
            for h in range(MINE):
                cells = jnp.concatenate([U[h, core], U[h, 2 + core]], axis=0)
                zero = jnp.zeros((2 * CELLS, 128), bf16)
                low, high = cells[:, :128], cells[:, 128:]
                w = W[h, pl.ds(i, 1)].reshape(plane, 256)
                attended += dot(jnp.where(left_two, zero, high), w[:, 128:], NT)
                values = jnp.concatenate([low, jnp.where(left_two, high, zero)], axis=1)
                normed += dot(values, w, NT)
            put(cols, (attended, normed))
            return 0
        lax.fori_loop(0, model // plane, chunk, 0)

    def core_copy():
        return remote(core_out, core_in, cs, cr, 4 * z + partner)

    def y_copy():
        return remote(y_out, y_in, ys, yr, 4 * z + across)

    def put_out(cols, both):
        for f in range(2):
            for yy in range(2):
                core_out[f, yy, :, cols] = both[f][yy * CELLS : (yy + 1) * CELLS].astype(bf16)

    def put_kept(cols, both):
        for f in range(2):
            for yy in range(2):
                kept[f, yy, :, cols] = both[f][yy * CELLS : (yy + 1) * CELLS]

    project(0)
    weights_arrived(3, 2)
    project(1)
    attend(0)
    project(2)
    attend(1)
    attend(2)
    weight_grads(0)
    weight_grads(1)
    weight_grads(2)
    line_step(0, 0)
    line_step(0, 1)
    results(1 - c, put_out)
    core_copy().start()
    line_step(0, 2)
    results(c, put_kept)
    core_copy().wait_recv()
    for f in range(2):
        y_out[f] = (kept[f, 1 - y] + core_in[f, 1 - y].astype(f32)).astype(bf16)
    y_copy().start()
    line_step(1, 0)
    line_step(1, 1)
    line_step(1, 2)
    line_step(0, 3)
    line_step(2, 0)
    line_step(2, 1)
    line_step(2, 2)
    line_step(1, 3)
    y_copy().wait_recv()
    done = [(kept[f, y] + core_in[f, y].astype(f32) + y_in[f].astype(f32)).astype(bf16) for f in range(2)]
    if lats > 1:
        for f in range(2):
            outs[0][f] = done[f]
    else:
        outs[0][...] = (stream[...].astype(f32) + done[0].astype(f32)).astype(bf16)
        outs[1][...] = (cot[...].astype(f32) + normalize_back(stream[...], gain[...], done[1])).astype(bf16)
    line_step(2, 3)

    for h in range(MINE):
        for k in (2, 1, 3):
            final_copy(h, k).wait_recv()
    for pair in range(2 * width // 256):
        for first in (0, 2):
            low, high = (
                F[head % MINE, head // MINE, :, 64 * first : 64 * first + 128].astype(f32) * factor
                for head in (2 * pair, 2 * pair + 1))
            a = jnp.where(left_d, low, pltpu.roll(high, 64, 1))
            b = jnp.where(left_d, pltpu.roll(low, 64, 1), high)
            out[:, first * width + 128 * pair : first * width + 128 * pair + 128] = a
            out[:, (first + 1) * width + 128 * pair : (first + 1) * width + 128 * pair + 128] = b

    for h in range(MINE):
        wp_copy(h).wait_send()
        wy_all(h, sent)
        wx_copy(h, z, x, True).wait_send()
        for k in (2, 1, 3):
            final_copy(h, k).wait_send()
        spread(h, z, sent, True, True)
        halo_copy(h).wait_send()
        edge_copy(h).wait_send()
        for i in range(last):
            z_copy(h, order[i], 0).wait_send()

    def weights_sent(zs, ways):
        for h in range(MINE):
            spread(h, zs, sent, **ways)
            wx_copy(h, zs, x).wait_send()

    for t in range(1, last + 1):
        from_planes(t, weights_sent)
    for f in range(2):
        for way in range(2):
            token_copy(f, way).wait_send()
        token_forward(f).wait_send()
    core_copy().wait_send()
    y_copy().wait_send()


def on_device(tokens, land, surface, gain, weights, shifts, index_table, bias_table, cotangent):
    levels, tile_rows, tile_cols, model = tokens.shape
    width = weights.shape[1] // 4
    count = levels * tile_rows * tile_cols
    lats = lax.axis_size("lat")
    n = lax.axis_size("lon")
    depth = model // n
    dma = pltpu.SemaphoreType.DMA

    if lats > 1:
        surface_term = jnp.where(land[None, :, :, None] == 1, surface[1], surface[0])
        stream = (tokens.astype(f32) + surface_term).astype(bf16)
        fields = jnp.stack([normalize(stream, gain), cotangent])
        below = passed_along(fields, "lat", -1)
        both = jnp.concatenate([fields, below], axis=2)
        fields = take_rows(both, shifts[:, 0], tile_rows)
        given = (fields.reshape(2, count, model),)
        specs = [VMEM]
        results = [jax.ShapeDtypeStruct((2, count, model), bf16)]
    else:
        given = (tokens.reshape(count, model), cotangent.reshape(count, model), land, surface, gain.reshape(1, model))
        specs = [VMEM] * 5
        results = [jax.ShapeDtypeStruct((count, model), bf16)] * 2

    factor = 1.0 / math.sqrt(count * lats * n)
    plane = MEMBERS * depth
    last = n // MEMBERS
    vm = pltpu.VMEM
    *back, grad_weights = pl.pallas_call(
        functools.partial(layer_kernel, width, n, lats, factor),
        name="layer",
        out_shape=(
            *results,
            jax.ShapeDtypeStruct((depth, 4 * width), f32),
        ),
        in_specs=[VMEM] + specs + [SMEM, VMEM, SMEM],
        out_specs=(VMEM,) * (len(results) + 1),
        scratch_shapes=[
            vm((MINE, count, count), f32),
            vm((count, model), bf16),
            vm((MEMBERS, MINE, depth, 256), bf16),
            vm((MINE, last, 2, 2, depth, 256), bf16),
            vm((2, MEMBERS, count, model), bf16),
            vm((2, model, MEMBERS * count), bf16),
            vm((MINE, MEMBERS + 1, count, 256), bf16),
            vm((MINE, MEMBERS, count, 256), bf16),
            vm((MINE, MEMBERS, count, 256), bf16),
            vm((MINE, count, 256), bf16),
            vm((MINE, count, 256), bf16),
            vm((MINE, last, plane, 256), bf16),
            vm((MINE, last, 2, plane, 256), bf16),
            vm((MINE, MEMBERS, depth, 256), bf16),
            vm((2, 2, count, model), f32),
            vm((2, 2, count, model), bf16),
            vm((2, 2, count, model), bf16),
            vm((2, count, model), bf16),
            vm((2, count, model), bf16),
            vm((count, 2 * count), bf16),
            vm((count, 2 * count), bf16),
            dma((MINE,)), dma((MINE,)), dma((MINE, 2)), dma((MINE,)),
            dma((MINE, last, 2)), dma((MINE, last)),
            dma((MINE, last)), dma((MINE, last)),
            dma((2, 2)), dma((2, 2)), dma((2,)), dma((2,)),
            dma((MINE,)), dma((MINE,)), dma((MINE,)), dma((MINE,)),
            dma((MINE, last)), dma((MINE, last, 2)),
            dma((MINE, 3)), dma((MINE, 3)),
            dma, dma, dma, dma,
        ],
        compiler_params=pltpu.CompilerParams(
            collective_id=0, has_side_effects=True, vmem_limit_bytes=60 * 2**20
        ),
        cost_estimate=pl.CostEstimate(flops=8 * 10**9, bytes_accessed=10 * 10**6, transcendentals=200000),
    )(weights, *given, bias_table, index_table, shifts)
    if lats == 1:
        return (back[0].reshape(tokens.shape), back[1].reshape(tokens.shape), grad_weights)
    back = back[0].reshape(2, levels, tile_rows, tile_cols, model)
    above = passed_along(back, "lat", 1)
    both = jnp.concatenate([above, back], axis=2)
    back = take_rows(both, tile_rows - shifts[:, 0], tile_rows)
    output = (stream.astype(f32) + back[0].astype(f32)).astype(bf16)
    grad_stream = normalize_back(stream, gain, back[1])
    grad_tokens = (cotangent.astype(f32) + grad_stream).astype(bf16)
    return (output, grad_tokens, lax.psum(grad_weights, "lat"))


def solution(mesh):
    return jax.shard_map(
        on_device,
        mesh=mesh,
        in_specs=(
            P("grp", "lat", "lon", None),
            P(("grp", "lat"), "lon"),
            P(),
            P(),
            P("lon", None),
            P(),
            P(),
            P("lat", None, None),
            P("grp", "lat", "lon", None),
        ),
        out_specs=(
            P("grp", "lat", "lon", None),
            P("grp", "lat", "lon", None),
            P(("grp", "lon"), None),
        ),
        check_vma=False,
    )
```

```python
import functools
import math

import jax
import jax.numpy as jnp
from jax import lax
from jax.experimental import pallas as pl
from jax.experimental.pallas import tpu as pltpu
from jax.sharding import PartitionSpec as P

epsilon = 1e-05
f32 = jnp.float32
bf16 = jnp.bfloat16
MESH = pl.DeviceIdType.MESH
ANY = pl.BlockSpec(memory_space=pl.ANY)
VMEM = pl.BlockSpec(memory_space=pltpu.VMEM)
SMEM = pl.BlockSpec(memory_space=pltpu.SMEM)
MEMBERS = 4
CELLS = 128
MINE = 3


def passed_along(shard, axis, by):
    count = lax.axis_size(axis)
    return lax.ppermute(shard, axis, [(i, (i + by) % count) for i in range(count)])


def dot(a, b, dims):
    return lax.dot_general(a, b, ((dims[0], dims[1]), ((), ())), preferred_element_type=f32)


NN = ((1,), (0,))
NT = ((1,), (1,))
TN = ((0,), (0,))


def normalize(stream, gain):
    values = stream.astype(f32)
    center = values - jnp.mean(values, axis=-1, keepdims=True)
    spread = lax.rsqrt(jnp.mean(center * center, axis=-1, keepdims=True) + epsilon)
    return (center * spread * gain).astype(bf16)


def normalize_back(stream, gain, grad_normed):
    values = stream.astype(f32)
    center = values - jnp.mean(values, axis=-1, keepdims=True)
    spread = lax.rsqrt(jnp.mean(center * center, axis=-1, keepdims=True) + epsilon)
    scaled = center * spread
    upstream = grad_normed.astype(f32) * gain
    return spread * (
        upstream
        - jnp.mean(upstream, axis=-1, keepdims=True)
        - scaled * jnp.mean(upstream * scaled, axis=-1, keepdims=True)
    )


def take_rows(both, starts, length):
    taken = both[:, :, :length]
    for start in range(1, length + 1):
        here = (starts == start)[None, :, None, None, None]
        taken = jnp.where(here, both[:, :, start : start + length], taken)
    return taken


def layer_kernel(width, n, lats, factor, *refs):
    if lats > 1:
        w_own, fields, table, index, shifts, *refs = refs
        outs, refs = refs[:2], refs[2:]
    else:
        w_own, tokens, cot, land, surface, gain, table, index, shifts, *refs = refs
        outs, refs = refs[:3], refs[3:]
    (bias, stream,
                 wown, W, X, XT, proj, G, U, edge, edge_in, gW, zbuf, F,
                 kept, core_out, core_in, y_out, y_in, roll_to, roll_from,
                 wps, wpr, wys, wyr, wzs, wzr, wxs, wxr, ts, tr, fs, fr, hs, hr, es, er,
                 zs_s, zs_r, gs_s, gs_r, cs, cr, ys, yr) = refs
    out = outs[-1]
    me = lax.axis_index("lon")
    x = lax.axis_index("grp")
    z, m = me // 4, me % 4
    y, c = m // 2, m % 2
    last = n // 4 - 1
    depth = w_own.shape[0]
    model = depth * n
    plane = 4 * depth
    partner, across = 2 * y + 1 - c, 2 * (1 - y) + c
    diag = 3 - m
    up, down = (me + 4) % n, (me + n - 4) % n

    def remote(src, dst, ssem, rsem, lon):
        return pltpu.make_async_remote_copy(
            src, dst, ssem, rsem, device_id={"lon": lon}, device_id_type=MESH)

    barrier = pltpu.get_barrier_semaphore()
    for k in range(1, 4):
        pl.semaphore_signal(barrier, inc=1, device_id={"lon": 4 * z + (m + k) % 4}, device_id_type=MESH)
    for lon in (up, down):
        pl.semaphore_signal(barrier, inc=1, device_id={"lon": lon}, device_id_type=MESH)
    pl.semaphore_signal(barrier, inc=1, device_id={"grp": 1 - x}, device_id_type=MESH)

    left = lax.broadcasted_iota(jnp.int32, (CELLS, 128), 1) < 64
    left_d = lax.broadcasted_iota(jnp.int32, (depth, 128), 1) < 64

    for pair in range(2 * width // 256):
        for first in (0, 2):
            a = w_own[:, first * width + 128 * pair : first * width + 128 * pair + 128].astype(f32)
            b = w_own[:, (first + 1) * width + 128 * pair : (first + 1) * width + 128 * pair + 128].astype(f32)
            low = jnp.where(left_d, a, pltpu.roll(b, 64, 1)).astype(bf16)
            high = jnp.where(left_d, pltpu.roll(a, 64, 1), b).astype(bf16)
            for head, value in ((2 * pair, low), (2 * pair + 1, high)):
                wown[head // MINE, head % MINE, :, 64 * first : 64 * first + 128] = value
    for h in range(MINE):
        W[h, z, y, c] = wown[m, h]
    if lats > 1:
        for f in range(2):
            X[f, m] = fields[f]
    else:
        X[1, m] = cot[...]

    pl.semaphore_wait(barrier, 6)

    def wp_copy(h):
        return remote(wown.at[partner, h], W.at[h, z, y, c], wps.at[h], wpr.at[h], 4 * z + partner)

    def wy_copy(h, core):
        to = 2 * (1 - y) + core
        return remote(wown.at[to, h], W.at[h, z, y, c], wys.at[h, core], wyr.at[h], 4 * z + to)

    def token_copy(f, way):
        to = across if way == 0 else partner
        return remote(X.at[f, m], X.at[f, m], ts.at[f, way], tr.at[f, way], 4 * z + to)

    def token_forward(f):
        return remote(X.at[f, across], X.at[f, across], fs.at[f], fr.at[f], 4 * z + partner)

    def wz_copy(h, zs, way):
        block = W.at[h, zs, :, x]
        to = up if way == 0 else down
        return remote(block, block, wzs.at[h, zs, way], wzr.at[h, zs], to)

    def wx_copy(h, zs, xx, here=False):
        block = W.at[h, zs, 1 - y, xx] if here else W.at[h, zs, :, xx]
        return pltpu.make_async_remote_copy(
            block, block, wxs.at[h, zs], wxr.at[h, zs], device_id={"grp": 1 - x}, device_id_type=MESH)

    def wy_all(h, act):
        def both():
            for core in range(2):
                act(wy_copy(h, core))
        pl.when(c == x)(both)

    start = lambda copy: copy.start()
    sent = lambda copy: copy.wait_send()
    for h in range(MINE):
        wp_copy(h).start()
        wy_all(h, start)
    for way in range(2):
        token_copy(1, way).start()
    if lats == 1:
        place = lax.broadcasted_iota(jnp.int32, (CELLS, 8), 0)
        spot = lax.broadcasted_iota(jnp.int32, (CELLS, 8), 1)
        row_hit = jnp.where(((place >> 3) & 7) == spot, 1.0, 0.0)
        marks = jnp.where((place & 7) == spot, dot(row_hit, land[...].astype(f32), NN), 0.0)
        on_land = jnp.sum(marks, axis=-1, keepdims=True) > 0.5
        term = jnp.where(on_land, surface[1:2, :], surface[0:1, :])
        stream[...] = (tokens[...].astype(f32) + term).astype(bf16)
        X[0, m] = normalize(stream[...], gain[...].reshape(1, model))
    for way in range(2):
        token_copy(0, way).start()

    lane = lax.broadcasted_iota(jnp.int32, (CELLS, 2 * CELLS), 1)
    cell = lax.broadcasted_iota(jnp.int32, (CELLS, 2 * CELLS), 0)

    def source(window_cell):
        lev, row, col = window_cell >> 6, (window_cell >> 3) & 7, window_cell & 7
        from_row = row
        if lats == 1:
            from_row = (row + jnp.where(lev == 0, shifts[0, 0], shifts[1, 0])) & 7
        from_col = col + jnp.where(lev == 0, shifts[0, 1], shifts[1, 1])
        return lev * 64 + from_row * 8 + (from_col & 7), from_col >= 8

    src, east = source(cell)
    roll_to[...] = jnp.where(src + jnp.where(east, CELLS, 0) == lane, 1.0, 0.0).astype(bf16)
    src, east = source(lane & 127)
    hit = (src == cell) & (jnp.where(east, 1, 0) == jnp.where(lane < CELLS, 1, 0))
    roll_from[...] = jnp.where(hit, 1.0, 0.0).astype(bf16)

    def spread(h, zs, act, to_up, to_down):
        if to_up:
            pl.when(z < last)(lambda: act(wz_copy(h, zs, 0)))
        if to_down:
            pl.when(z > 0)(lambda: act(wz_copy(h, zs, 1)))


    def transpose(t):
        for f in range(2):
            def chunk(i, _):
                cols = pl.ds(pl.multiple_of(i * 512, 512), 512)
                XT[f, cols, pl.ds(pl.multiple_of(t * CELLS, CELLS), CELLS)] = (
                    X[f, t, :, cols].astype(f32).T.astype(bf16))
                return 0
            lax.fori_loop(0, model // 512, chunk, 0)

    def from_planes(t, act):
        pl.when(z - t >= 0)(lambda: act(z - t, dict(to_up=True, to_down=False)))
        pl.when(z + t <= last)(lambda: act(z + t, dict(to_up=False, to_down=True)))

    def make_bias():
        area = CELLS // 2
        half = lax.broadcasted_iota(jnp.int32, (area, CELLS), 1) < area
        entry = jnp.concatenate([index[...], index[...]], axis=1)
        unroll = next(u for u in (5, 3, 1) if table.shape[2] % u == 0)

        def some(i, found):
            for u in range(unroll):
                r = i * unroll + u
                here = entry == r
                found = tuple(
                    jnp.where(here, jnp.where(half, table[MINE * m + h, 0, r], table[MINE * m + h, 1, r]), found[h])
                    for h in range(MINE))
            return found

        found = lax.fori_loop(
            0, table.shape[2] // unroll, some, tuple(jnp.zeros((area, CELLS), f32) for _ in range(MINE)))
        query = lax.broadcasted_iota(jnp.int32, (area, CELLS), 0) >> 3
        key = (lax.broadcasted_iota(jnp.int32, (area, CELLS), 1) & 63) >> 3
        first_row = 0 if lats == 1 else 8 * lax.axis_index("lat")
        for lev in range(2):
            edge_row = 8 * lats - shifts[lev, 0] - first_row
            same = jnp.where(query >= edge_row, 1, 0) == jnp.where(key >= edge_row, 1, 0)
            keep = half if lev == 0 else jnp.logical_not(half)
            for h in range(MINE):
                masked = jnp.where(same, found[h], -1e30)
                bias[h, lev * area : (lev + 1) * area, :] = jnp.where(keep, masked, -jnp.inf)

    def weights_arrived(t, h):
        if t == 0:
            wp_copy(h).wait_recv()
            wy_copy(h, 0).wait_recv()
            spread(h, z, start, True, True)
            wx_copy(h, z, x, True).start()
            return

        def arrived(zs, ways):
            wz_copy(h, zs, 0).wait_recv()
            spread(h, zs, start, **ways)
            wx_copy(h, zs, x).start()
        from_planes(t, arrived)

    def tokens_across(f):
        token_copy(f, 0).wait_recv()
        token_forward(f).start()

    weights_arrived(0, 0)
    weights_arrived(1, 0)
    weights_arrived(0, 1)
    transpose(m)
    weights_arrived(2, 0)
    weights_arrived(1, 1)
    weights_arrived(0, 2)
    make_bias()
    for f in range(2):
        token_copy(f, 1).wait_recv()
    transpose(partner)
    weights_arrived(3, 0)
    tokens_across(1)
    weights_arrived(2, 1)
    weights_arrived(1, 2)
    weights_arrived(3, 1)
    tokens_across(0)
    weights_arrived(2, 2)
    transpose(across)
    for f in range(2):
        token_forward(f).wait_recv()
    transpose(diag)

    def halo_copy(h):
        return remote(proj.at[h, 0], proj.at[h, MEMBERS], hs.at[h], hr.at[h], down)

    left_all = lax.broadcasted_iota(jnp.int32, (MEMBERS * CELLS, 128), 1) < 64

    def project(h):
        def wait_x(zs, ways):
            wx_copy(h, zs, 1 - x).wait_recv()
        wx_copy(h, z, 1 - x, True).wait_recv()
        for t in range(1, last + 1):
            from_planes(t, wait_x)
        w = W[h].reshape(model, 256)
        normed = dot(X[0].reshape(MEMBERS * CELLS, model), w, NN)
        grads = dot(X[1].reshape(MEMBERS * CELLS, model), w[:, 128:], NN)
        high = jnp.where(left_all, normed[:, 128:], grads)
        proj[h, :MEMBERS, :, :128] = normed[:, :128].astype(bf16).reshape(MEMBERS, CELLS, 128)
        proj[h, :MEMBERS, :, 128:] = high.astype(bf16).reshape(MEMBERS, CELLS, 128)
        halo_copy(h).start()

    def windows(h, which):
        each = range(len(which))
        zero = jnp.zeros((CELLS, 128), bf16)
        rolled = [dot(roll_to[...], proj[h, w : w + 2].reshape(2 * CELLS, 256), NN) for w in which]
        swapped = [(pltpu.roll(r[:, :128], 64, 1).astype(bf16), pltpu.roll(r[:, 128:], 64, 1).astype(bf16)) for r in rolled]
        q = [jnp.where(left, r[:, :128].astype(bf16), zero) for r in rolled]
        g = [jnp.where(left, zero, r[:, 128:].astype(bf16)) for r in rolled]
        kv = [jnp.where(left, kq, gv) for kq, gv in swapped]
        both = [dot(jnp.concatenate([q[i], g[i]], axis=0), kv[i], NT) for i in each]
        s = [a[:CELLS] * 0.125 + bias[h] for a in both]
        grad_probs = [a[CELLS:] for a in both]
        top = [jnp.max(a, axis=-1, keepdims=True) for a in s]
        expo = [jnp.exp(s[i] - top[i]) for i in each]
        total = [jnp.sum(a, axis=-1, keepdims=True) for a in expo]
        probs = [expo[i] / total[i] for i in each]
        probs_b = [a.astype(bf16) for a in probs]
        inner = [jnp.sum(probs[i] * grad_probs[i], axis=-1, keepdims=True) for i in each]
        gs = [(probs[i] * (grad_probs[i] - inner[i]) * 0.125).astype(bf16) for i in each]
        low = [dot(jnp.concatenate([gs[i], gs[i].T], axis=0), swapped[i][0], NN) for i in each]
        high = [dot(jnp.concatenate([probs_b[i].T, probs_b[i]], axis=0), swapped[i][1], NN) for i in each]
        for i in each:
            G[h, which[i], :, :128] = jnp.where(left, low[i][:CELLS], low[i][CELLS:]).astype(bf16)
            G[h, which[i], :, 128:] = jnp.where(left, high[i][:CELLS], high[i][CELLS:]).astype(bf16)

    def edge_copy(h):
        return remote(edge.at[h], edge_in.at[h], es.at[h], er.at[h], up)

    def attend(h):
        halo_copy(h).wait_recv()
        windows(h, list(range(MEMBERS)))
        edge[h] = dot(roll_from[:, :CELLS], G[h, MEMBERS - 1], NN).astype(bf16)
        edge_copy(h).start()
        for t in range(1, MEMBERS):
            U[h, t] = dot(roll_from[...], G[h, t - 1 : t + 1].reshape(2 * CELLS, 256), NN).astype(bf16)

    order = [3 - 3 * (z // 2), 2 - z // 2, (5 - z) % 4, z]

    def finish_cells(h):
        edge_copy(h).wait_recv()
        own = dot(roll_from[:, CELLS:], G[h, 0], NN)
        U[h, 0] = (own + edge_in[h].astype(f32)).astype(bf16)

    def weight_grads(h):
        all_cells = U[h].reshape(MEMBERS * CELLS, 256)
        left_p = lax.broadcasted_iota(jnp.int32, (plane, 128), 1) < 64
        for d in order:
            rows = pl.ds(pl.multiple_of(d * plane, plane), plane)
            first = dot(XT[0, rows, :], all_cells, NN)
            second = dot(XT[1, rows, :], all_cells[:, 128:], NN)
            gW[h, d, :, :128] = first[:, :128].astype(bf16)
            gW[h, d, :, 128:] = jnp.where(left_p, first[:, 128:], second).astype(bf16)

    def z_copy(h, d, way):
        return remote(gW.at[h, d], zbuf.at[h, d, way], zs_s.at[h, d], zs_r.at[h, d, way],
                      up if way == 0 else down)

    def end_send(h, i):
        pl.when(z == 0)(lambda: z_copy(h, order[i], 0).start())
        pl.when(z == last)(lambda: z_copy(h, order[i], 1).start())

    def add(h, d, *ways):
        total = gW[h, d].astype(f32)
        for way in ways:
            total += zbuf[h, d, way].astype(f32)
        gW[h, d] = total.astype(bf16)

    def final_copy(h, k):
        to = (m + k) % 4
        rows = pl.ds(pl.multiple_of(to * depth, depth), depth)
        return remote(gW.at[h, z, rows], F.at[h, m], gs_s.at[h, k - 1], gs_r.at[h, k - 1], 4 * z + to)

    def line_step(h, i):
        d = order[i]

        def go_up():
            z_copy(h, d, 0).wait_recv()
            add(h, d, 0)
            z_copy(h, d, 0).start()

        def go_down():
            z_copy(h, d, 1).wait_recv()
            add(h, d, 1)
            z_copy(h, d, 1).start()

        if i < last:
            pl.when((d > z) & (z > 0))(go_up)
            pl.when((d < z) & (z < last))(go_down)
            return

        def from_below():
            z_copy(h, d, 0).wait_recv()
            add(h, d, 0)

        def from_above():
            z_copy(h, d, 1).wait_recv()
            add(h, d, 1)
        pl.when(z > 0)(from_below)
        pl.when(z < last)(from_above)
        for k in (2, 1, 3):
            final_copy(h, k).start()
        F[h, m] = gW[h, z, pl.ds(pl.multiple_of(m * depth, depth), depth), :]

    def results(core, put):
        left_two = lax.broadcasted_iota(jnp.int32, (2 * CELLS, 128), 1) < 64

        def chunk(i, _):
            cols = pl.ds(pl.multiple_of(i * plane, plane), plane)
            attended = jnp.zeros((2 * CELLS, plane), f32)
            normed = jnp.zeros((2 * CELLS, plane), f32)
            for h in range(MINE):
                cells = jnp.concatenate([U[h, core], U[h, 2 + core]], axis=0)
                zero = jnp.zeros((2 * CELLS, 128), bf16)
                low, high = cells[:, :128], cells[:, 128:]
                w = W[h, pl.ds(i, 1)].reshape(plane, 256)
                attended += dot(jnp.where(left_two, zero, high), w[:, 128:], NT)
                values = jnp.concatenate([low, jnp.where(left_two, high, zero)], axis=1)
                normed += dot(values, w, NT)
            put(cols, (attended, normed))
            return 0
        lax.fori_loop(0, model // plane, chunk, 0)

    def core_copy():
        return remote(core_out, core_in, cs, cr, 4 * z + partner)

    def y_copy():
        return remote(y_out, y_in, ys, yr, 4 * z + across)

    def put_out(cols, both):
        for f in range(2):
            for yy in range(2):
                core_out[f, yy, :, cols] = both[f][yy * CELLS : (yy + 1) * CELLS].astype(bf16)

    def put_kept(cols, both):
        for f in range(2):
            for yy in range(2):
                kept[f, yy, :, cols] = both[f][yy * CELLS : (yy + 1) * CELLS]

    def assemble(h):
        for k in (2, 1, 3):
            final_copy(h, k).wait_recv()
        for member in range(MEMBERS):
            for block in range(4):
                at = block * width + 64 * (MINE * member + h)
                out[:, at : at + 64] = F[h, member, :, 64 * block : 64 * block + 64].astype(f32) * factor

    def finish_fields():
        y_copy().wait_recv()
        done = [(kept[f, y] + core_in[f, y].astype(f32) + y_in[f].astype(f32)).astype(bf16) for f in range(2)]
        if lats > 1:
            for f in range(2):
                outs[0][f] = done[f]
        else:
            outs[0][...] = (stream[...].astype(f32) + done[0].astype(f32)).astype(bf16)
            grad_stream = normalize_back(stream[...], gain[...].reshape(1, model), done[1])
            outs[1][...] = (cot[...].astype(f32) + grad_stream).astype(bf16)

    project(0)
    weights_arrived(3, 2)
    project(1)
    attend(0)
    project(2)
    attend(1)
    attend(2)
    finish_cells(0)
    weight_grads(0)
    for i in range(last):
        end_send(0, i)
    finish_cells(1)
    finish_cells(2)
    results(1 - c, put_out)
    core_copy().start()
    weight_grads(1)
    for i in range(last):
        end_send(1, i)
    results(c, put_kept)
    core_copy().wait_recv()
    for f in range(2):
        y_out[f] = (kept[f, 1 - y] + core_in[f, 1 - y].astype(f32)).astype(bf16)
    y_copy().start()
    weight_grads(2)
    for i in range(last):
        end_send(2, i)
    line_step(0, 0)
    line_step(0, 1)
    line_step(0, 2)
    line_step(0, 3)
    for i in range(last):
        line_step(1, i)
    assemble(0)
    line_step(1, 3)
    line_step(2, 0)
    line_step(2, 1)
    finish_fields()
    line_step(2, 2)
    assemble(1)
    line_step(2, 3)
    assemble(2)

    for h in range(MINE):
        wp_copy(h).wait_send()
        wy_all(h, sent)
        wx_copy(h, z, x, True).wait_send()
        for k in (2, 1, 3):
            final_copy(h, k).wait_send()
        spread(h, z, sent, True, True)
        halo_copy(h).wait_send()
        edge_copy(h).wait_send()
        for i in range(last):
            z_copy(h, order[i], 0).wait_send()

    def weights_sent(zs, ways):
        for h in range(MINE):
            spread(h, zs, sent, **ways)
            wx_copy(h, zs, x).wait_send()

    for t in range(1, last + 1):
        from_planes(t, weights_sent)
    for f in range(2):
        for way in range(2):
            token_copy(f, way).wait_send()
        token_forward(f).wait_send()
    core_copy().wait_send()
    y_copy().wait_send()


def hand_over(*refs):
    count = len(refs) // 3
    copies = [pltpu.make_async_copy(refs[i], refs[count + i], refs[2 * count + i]) for i in range(count)]
    for copy in copies:
        copy.start()
    for copy in copies:
        copy.wait()


def on_device(tokens, land, surface, gain, weights, shifts, index_table, bias_table, cotangent):
    levels, tile_rows, tile_cols, model = tokens.shape
    width = weights.shape[1] // 4
    count = levels * tile_rows * tile_cols
    lats = lax.axis_size("lat")
    n = lax.axis_size("lon")
    depth = model // n
    dma = pltpu.SemaphoreType.DMA

    if lats > 1:
        surface_term = jnp.where(land[None, :, :, None] == 1, surface[1], surface[0])
        stream = (tokens.astype(f32) + surface_term).astype(bf16)
        fields = jnp.stack([normalize(stream, gain), cotangent])
        below = passed_along(fields, "lat", -1)
        both = jnp.concatenate([fields, below], axis=2)
        fields = take_rows(both, shifts[:, 0], tile_rows)
        given = (fields.reshape(2, count, model),)
        specs = [VMEM]
        results = [jax.ShapeDtypeStruct((2, count, model), bf16)]
    else:
        given = (tokens.reshape(count, model), cotangent.reshape(count, model), land, surface, gain)
        specs = [VMEM] * 5
        results = [jax.ShapeDtypeStruct((count, model), bf16)] * 2

    factor = 1.0 / math.sqrt(count * lats * n)
    plane = MEMBERS * depth
    last = n // MEMBERS
    vm = pltpu.VMEM
    *back, grad_weights = pl.pallas_call(
        functools.partial(layer_kernel, width, n, lats, factor),
        name="layer",
        out_shape=(
            *results,
            jax.ShapeDtypeStruct((depth, 4 * width), f32),
        ),
        in_specs=[VMEM] + specs + [SMEM, VMEM, SMEM],
        out_specs=(VMEM,) * (len(results) + 1),
        scratch_shapes=[
            vm((MINE, count, count), f32),
            vm((count, model), bf16),
            vm((MEMBERS, MINE, depth, 256), bf16),
            vm((MINE, last, 2, 2, depth, 256), bf16),
            vm((2, MEMBERS, count, model), bf16),
            vm((2, model, MEMBERS * count), bf16),
            vm((MINE, MEMBERS + 1, count, 256), bf16),
            vm((MINE, MEMBERS, count, 256), bf16),
            vm((MINE, MEMBERS, count, 256), bf16),
            vm((MINE, count, 256), bf16),
            vm((MINE, count, 256), bf16),
            vm((MINE, last, plane, 256), bf16),
            vm((MINE, last, 2, plane, 256), bf16),
            vm((MINE, MEMBERS, depth, 256), bf16),
            vm((2, 2, count, model), f32),
            vm((2, 2, count, model), bf16),
            vm((2, 2, count, model), bf16),
            vm((2, count, model), bf16),
            vm((2, count, model), bf16),
            vm((count, 2 * count), bf16),
            vm((count, 2 * count), bf16),
            dma((MINE,)), dma((MINE,)), dma((MINE, 2)), dma((MINE,)),
            dma((MINE, last, 2)), dma((MINE, last)),
            dma((MINE, last)), dma((MINE, last)),
            dma((2, 2)), dma((2, 2)), dma((2,)), dma((2,)),
            dma((MINE,)), dma((MINE,)), dma((MINE,)), dma((MINE,)),
            dma((MINE, last)), dma((MINE, last, 2)),
            dma((MINE, 3)), dma((MINE, 3)),
            dma, dma, dma, dma,
        ],
        compiler_params=pltpu.CompilerParams(
            collective_id=0, has_side_effects=True, vmem_limit_bytes=60 * 2**20
        ),
        cost_estimate=pl.CostEstimate(flops=8 * 10**9, bytes_accessed=10 * 10**6, transcendentals=200000),
    )(weights, *given, bias_table.transpose(2, 0, 1), index_table, shifts)
    if lats == 1:
        made = (*back, grad_weights)
        made = pl.pallas_call(
            hand_over,
            name="hand_over",
            out_shape=tuple(jax.ShapeDtypeStruct(a.shape, a.dtype) for a in made),
            in_specs=[VMEM] * 3,
            out_specs=(ANY,) * 3,
            scratch_shapes=[dma] * 3,
            cost_estimate=pl.CostEstimate(flops=0, bytes_accessed=4 * 10**6, transcendentals=0),
        )(*made)
        return (made[0].reshape(tokens.shape), made[1].reshape(tokens.shape), made[2])
    back = back[0].reshape(2, levels, tile_rows, tile_cols, model)
    above = passed_along(back, "lat", 1)
    both = jnp.concatenate([above, back], axis=2)
    back = take_rows(both, tile_rows - shifts[:, 0], tile_rows)
    output = (stream.astype(f32) + back[0].astype(f32)).astype(bf16)
    grad_stream = normalize_back(stream, gain, back[1])
    grad_tokens = (cotangent.astype(f32) + grad_stream).astype(bf16)
    return (output, grad_tokens, lax.psum(grad_weights, "lat"))


def solution(mesh):
    return jax.shard_map(
        on_device,
        mesh=mesh,
        in_specs=(
            P("grp", "lat", "lon", None),
            P(("grp", "lat"), "lon"),
            P(),
            P(),
            P("lon", None),
            P(),
            P(),
            P("lat", None, None),
            P("grp", "lat", "lon", None),
        ),
        out_specs=(
            P("grp", "lat", "lon", None),
            P("grp", "lat", "lon", None),
            P(("grp", "lon"), None),
        ),
        check_vma=False,
    )
```

```python
import functools
import math

import jax
import jax.numpy as jnp
from jax import lax
from jax.experimental import pallas as pl
from jax.experimental.pallas import tpu as pltpu
from jax.sharding import PartitionSpec as P

epsilon = 1e-05
f32 = jnp.float32
bf16 = jnp.bfloat16
MESH = pl.DeviceIdType.MESH
ANY = pl.BlockSpec(memory_space=pl.ANY)
VMEM = pl.BlockSpec(memory_space=pltpu.VMEM)
SMEM = pl.BlockSpec(memory_space=pltpu.SMEM)
MEMBERS = 4
CELLS = 128
MINE = 3


def passed_along(shard, axis, by):
    count = lax.axis_size(axis)
    return lax.ppermute(shard, axis, [(i, (i + by) % count) for i in range(count)])


def dot(a, b, dims):
    return lax.dot_general(a, b, ((dims[0], dims[1]), ((), ())), preferred_element_type=f32)


NN = ((1,), (0,))
NT = ((1,), (1,))
TN = ((0,), (0,))


def normalize(stream, gain):
    values = stream.astype(f32)
    center = values - jnp.mean(values, axis=-1, keepdims=True)
    spread = lax.rsqrt(jnp.mean(center * center, axis=-1, keepdims=True) + epsilon)
    return (center * spread * gain).astype(bf16)


def normalize_back(stream, gain, grad_normed):
    values = stream.astype(f32)
    center = values - jnp.mean(values, axis=-1, keepdims=True)
    spread = lax.rsqrt(jnp.mean(center * center, axis=-1, keepdims=True) + epsilon)
    scaled = center * spread
    upstream = grad_normed.astype(f32) * gain
    return spread * (
        upstream
        - jnp.mean(upstream, axis=-1, keepdims=True)
        - scaled * jnp.mean(upstream * scaled, axis=-1, keepdims=True)
    )


def take_rows(both, starts, length):
    taken = both[:, :, :length]
    for start in range(1, length + 1):
        here = (starts == start)[None, :, None, None, None]
        taken = jnp.where(here, both[:, :, start : start + length], taken)
    return taken


def layer_kernel(width, n, lats, factor, *refs):
    if lats > 1:
        w_own, fields, table, index, shifts, *refs = refs
        outs, refs = refs[:2], refs[2:]
    else:
        w_own, tokens, cot, land, surface, gain, table, index, shifts, *refs = refs
        outs, refs = refs[:3], refs[3:]
    (bias, stream, far_x, far_xt, far_u, fxs, fxr, fps, fpr, fus, fur,
                 wown, W, X, XT, proj, G, U, edge, edge_in, gW, zbuf, F,
                 kept, core_out, core_in, y_out, y_in, roll_to, roll_from,
                 wps, wpr, wys, wyr, wzs, wzr, wxs, wxr, ts, tr, fs, fr, hs, hr, es, er,
                 zs_s, zs_r, gs_s, gs_r, cs, cr, ys, yr) = refs
    out = outs[-1]
    me = lax.axis_index("lon")
    x = lax.axis_index("grp")
    z, m = me // 4, me % 4
    y, c = m // 2, m % 2
    last = n // 4 - 1
    depth = w_own.shape[0]
    model = depth * n
    plane = 4 * depth
    partner, across = 2 * y + 1 - c, 2 * (1 - y) + c
    diag = 3 - m
    up, down = (me + 4) % n, (me + n - 4) % n

    def remote(src, dst, ssem, rsem, lon):
        return pltpu.make_async_remote_copy(
            src, dst, ssem, rsem, device_id={"lon": lon}, device_id_type=MESH)

    barrier = pltpu.get_barrier_semaphore()
    for k in range(1, 4):
        pl.semaphore_signal(barrier, inc=1, device_id={"lon": 4 * z + (m + k) % 4}, device_id_type=MESH)
    for lon in (up, down):
        pl.semaphore_signal(barrier, inc=1, device_id={"lon": lon}, device_id_type=MESH)
    pl.semaphore_signal(barrier, inc=1, device_id={"grp": 1 - x}, device_id_type=MESH)

    left = lax.broadcasted_iota(jnp.int32, (CELLS, 128), 1) < 64
    left_d = lax.broadcasted_iota(jnp.int32, (depth, 128), 1) < 64

    for pair in range(2 * width // 256):
        for first in (0, 2):
            a = w_own[:, first * width + 128 * pair : first * width + 128 * pair + 128].astype(f32)
            b = w_own[:, (first + 1) * width + 128 * pair : (first + 1) * width + 128 * pair + 128].astype(f32)
            low = jnp.where(left_d, a, pltpu.roll(b, 64, 1)).astype(bf16)
            high = jnp.where(left_d, pltpu.roll(a, 64, 1), b).astype(bf16)
            for head, value in ((2 * pair, low), (2 * pair + 1, high)):
                wown[head // MINE, head % MINE, :, 64 * first : 64 * first + 128] = value
    for h in range(MINE):
        W[h, z, y, c] = wown[m, h]
    if lats > 1:
        for f in range(2):
            X[f, m] = fields[f]
    else:
        X[1, m] = cot[...]

    pl.semaphore_wait(barrier, 6)

    def wp_copy(h):
        return remote(wown.at[partner, h], W.at[h, z, y, c], wps.at[h], wpr.at[h], 4 * z + partner)

    def wy_copy(h, core):
        to = 2 * (1 - y) + core
        return remote(wown.at[to, h], W.at[h, z, y, c], wys.at[h, core], wyr.at[h], 4 * z + to)

    def token_copy(f, way):
        to = across if way == 0 else partner
        return remote(X.at[f, m], X.at[f, m], ts.at[f, way], tr.at[f, way], 4 * z + to)

    def token_forward(f):
        return remote(X.at[f, across], X.at[f, across], fs.at[f], fr.at[f], 4 * z + partner)

    def wz_copy(h, zs, way):
        block = W.at[h, zs, :, x]
        to = up if way == 0 else down
        return remote(block, block, wzs.at[h, zs, way], wzr.at[h, zs], to)

    def wx_copy(h, zs, xx, here=False):
        block = W.at[h, zs, 1 - y, xx] if here else W.at[h, zs, :, xx]
        return pltpu.make_async_remote_copy(
            block, block, wxs.at[h, zs], wxr.at[h, zs], device_id={"grp": 1 - x}, device_id_type=MESH)

    def wy_all(h, act):
        def both():
            for core in range(2):
                act(wy_copy(h, core))
        pl.when(c == x)(both)

    start = lambda copy: copy.start()
    sent = lambda copy: copy.wait_send()
    for h in range(MINE):
        wp_copy(h).start()
        wy_all(h, start)
    for way in range(2):
        token_copy(1, way).start()
    if lats == 1:
        place = lax.broadcasted_iota(jnp.int32, (CELLS, 8), 0)
        spot = lax.broadcasted_iota(jnp.int32, (CELLS, 8), 1)
        row_hit = jnp.where(((place >> 3) & 7) == spot, 1.0, 0.0)
        marks = jnp.where((place & 7) == spot, dot(row_hit, land[...].astype(f32), NN), 0.0)
        on_land = jnp.sum(marks, axis=-1, keepdims=True) > 0.5
        term = jnp.where(on_land, surface[1:2, :], surface[0:1, :])
        stream[...] = (tokens[...].astype(f32) + term).astype(bf16)
        X[0, m] = normalize(stream[...], gain[...].reshape(1, model))
    for way in range(2):
        token_copy(0, way).start()

    lane = lax.broadcasted_iota(jnp.int32, (CELLS, 2 * CELLS), 1)
    cell = lax.broadcasted_iota(jnp.int32, (CELLS, 2 * CELLS), 0)

    def source(window_cell):
        lev, row, col = window_cell >> 6, (window_cell >> 3) & 7, window_cell & 7
        from_row = row
        if lats == 1:
            from_row = (row + jnp.where(lev == 0, shifts[0, 0], shifts[1, 0])) & 7
        from_col = col + jnp.where(lev == 0, shifts[0, 1], shifts[1, 1])
        return lev * 64 + from_row * 8 + (from_col & 7), from_col >= 8

    src, east = source(cell)
    roll_to[...] = jnp.where(src + jnp.where(east, CELLS, 0) == lane, 1.0, 0.0).astype(bf16)
    src, east = source(lane & 127)
    hit = (src == cell) & (jnp.where(east, 1, 0) == jnp.where(lane < CELLS, 1, 0))
    roll_from[...] = jnp.where(hit, 1.0, 0.0).astype(bf16)

    def spread(h, zs, act, to_up, to_down):
        if to_up:
            pl.when(z < last)(lambda: act(wz_copy(h, zs, 0)))
        if to_down:
            pl.when(z > 0)(lambda: act(wz_copy(h, zs, 1)))


    def transpose(t):
        for f in range(2):
            def chunk(i, _):
                cols = pl.ds(pl.multiple_of(i * 512, 512), 512)
                XT[f, cols, pl.ds(pl.multiple_of(t * CELLS, CELLS), CELLS)] = (
                    X[f, t, :, cols].astype(f32).T.astype(bf16))
                return 0
            lax.fori_loop(0, model // 512, chunk, 0)

    def from_planes(t, act):
        pl.when(z - t >= 0)(lambda: act(z - t, dict(to_up=True, to_down=False)))
        pl.when(z + t <= last)(lambda: act(z + t, dict(to_up=False, to_down=True)))

    def make_bias():
        area = CELLS // 2
        half = lax.broadcasted_iota(jnp.int32, (area, CELLS), 1) < area
        entry = jnp.concatenate([index[...], index[...]], axis=1)
        unroll = next(u for u in (5, 3, 1) if table.shape[2] % u == 0)

        def some(i, found):
            for u in range(unroll):
                r = i * unroll + u
                here = entry == r
                found = tuple(
                    jnp.where(here, jnp.where(half, table[MINE * m + h, 0, r], table[MINE * m + h, 1, r]), found[h])
                    for h in range(MINE))
            return found

        found = lax.fori_loop(
            0, table.shape[2] // unroll, some, tuple(jnp.zeros((area, CELLS), f32) for _ in range(MINE)))
        query = lax.broadcasted_iota(jnp.int32, (area, CELLS), 0) >> 3
        key = (lax.broadcasted_iota(jnp.int32, (area, CELLS), 1) & 63) >> 3
        first_row = 0 if lats == 1 else 8 * lax.axis_index("lat")
        for lev in range(2):
            edge_row = 8 * lats - shifts[lev, 0] - first_row
            same = jnp.where(query >= edge_row, 1, 0) == jnp.where(key >= edge_row, 1, 0)
            keep = half if lev == 0 else jnp.logical_not(half)
            for h in range(MINE):
                masked = jnp.where(same, found[h], -1e30)
                bias[h, lev * area : (lev + 1) * area, :] = jnp.where(keep, masked, -jnp.inf)

    def weights_arrived(t, h):
        if t == 0:
            wp_copy(h).wait_recv()
            wy_copy(h, 0).wait_recv()
            spread(h, z, start, True, True)
            wx_copy(h, z, x, True).start()
            return

        def arrived(zs, ways):
            wz_copy(h, zs, 0).wait_recv()
            spread(h, zs, start, **ways)
            wx_copy(h, zs, x).start()
        from_planes(t, arrived)

    half_model = model // 2
    middle = (z > 0) & (z < last)

    def far_tile(which):
        return m if which == 0 else across

    def far_copy(f, which, bottom):
        t = far_tile(which)
        cols = pl.ds(half_model if bottom else 0, half_model)
        return remote(X.at[f, t, :, cols], far_x.at[f, t], fxs.at[f, which], fxr.at[f, which], up if bottom else down)

    def far_send(f, which, act):
        pl.when(z == 0)(lambda: act(far_copy(f, which, True)))
        pl.when(z == last)(lambda: act(far_copy(f, which, False)))

    def far_pass(f, which):
        block = far_x.at[f, far_tile(which)]
        return remote(block, block, fps.at[f, which], fpr.at[f, which], 4 * z + partner)

    def far_transpose(f, t):
        for i in range(model // 2 // 256):
            rows = pl.ds(i * 256, 256)
            far_xt[f, rows, pl.ds(pl.multiple_of(t * CELLS, CELLS), CELLS)] = (
                far_x[f, t, :, rows].astype(f32).T.astype(bf16))

    def far_y(f):
        return remote(far_x.at[f, m], far_x.at[f, m], fxs.at[f, 1], fxr.at[f, 1], 4 * z + across)

    def far_own():
        for f in (1, 0):
            far_copy(f, 0, True).wait_recv()
            far_pass(f, 0).start()
            far_y(f).start()

    def far_first():
        for f in (1, 0):
            far_transpose(f, m)
        for f in (1, 0):
            far_pass(f, 0).wait_recv()
            far_transpose(f, partner)

    def far_second():
        for f in (1, 0):
            far_y(f).wait_recv()
            far_pass(f, 1).start()
            far_transpose(f, across)
        for f in (1, 0):
            far_pass(f, 1).wait_recv()
            far_transpose(f, diag)

    def tokens_across(f):
        token_copy(f, 0).wait_recv()
        token_forward(f).start()

    weights_arrived(0, 0)
    weights_arrived(1, 0)
    weights_arrived(0, 1)
    transpose(m)
    weights_arrived(2, 0)
    weights_arrived(1, 1)
    weights_arrived(0, 2)
    for f in (1, 0):
        far_send(f, 0, start)
    make_bias()
    for f in range(2):
        token_copy(f, 1).wait_recv()
    transpose(partner)
    weights_arrived(3, 0)
    tokens_across(1)
    weights_arrived(2, 1)
    weights_arrived(1, 2)
    weights_arrived(3, 1)
    tokens_across(0)
    pl.when(middle)(far_own)
    weights_arrived(2, 2)
    transpose(across)
    for f in range(2):
        token_forward(f).wait_recv()
    transpose(diag)

    def halo_copy(h):
        return remote(proj.at[h, 0], proj.at[h, MEMBERS], hs.at[h], hr.at[h], down)

    left_all = lax.broadcasted_iota(jnp.int32, (MEMBERS * CELLS, 128), 1) < 64

    def project(h):
        def wait_x(zs, ways):
            wx_copy(h, zs, 1 - x).wait_recv()
        wx_copy(h, z, 1 - x, True).wait_recv()
        for t in range(1, last + 1):
            from_planes(t, wait_x)
        w = W[h].reshape(model, 256)
        normed = dot(X[0].reshape(MEMBERS * CELLS, model), w, NN)
        grads = dot(X[1].reshape(MEMBERS * CELLS, model), w[:, 128:], NN)
        high = jnp.where(left_all, normed[:, 128:], grads)
        proj[h, :MEMBERS, :, :128] = normed[:, :128].astype(bf16).reshape(MEMBERS, CELLS, 128)
        proj[h, :MEMBERS, :, 128:] = high.astype(bf16).reshape(MEMBERS, CELLS, 128)
        halo_copy(h).start()

    def windows(h, which):
        each = range(len(which))
        zero = jnp.zeros((CELLS, 128), bf16)
        rolled = [dot(roll_to[...], proj[h, w : w + 2].reshape(2 * CELLS, 256), NN) for w in which]
        swapped = [(pltpu.roll(r[:, :128], 64, 1).astype(bf16), pltpu.roll(r[:, 128:], 64, 1).astype(bf16)) for r in rolled]
        q = [jnp.where(left, r[:, :128].astype(bf16), zero) for r in rolled]
        g = [jnp.where(left, zero, r[:, 128:].astype(bf16)) for r in rolled]
        kv = [jnp.where(left, kq, gv) for kq, gv in swapped]
        both = [dot(jnp.concatenate([q[i], g[i]], axis=0), kv[i], NT) for i in each]
        s = [a[:CELLS] * 0.125 + bias[h] for a in both]
        grad_probs = [a[CELLS:] for a in both]
        top = [jnp.max(a, axis=-1, keepdims=True) for a in s]
        expo = [jnp.exp(s[i] - top[i]) for i in each]
        total = [jnp.sum(a, axis=-1, keepdims=True) for a in expo]
        probs = [expo[i] / total[i] for i in each]
        probs_b = [a.astype(bf16) for a in probs]
        inner = [jnp.sum(probs[i] * grad_probs[i], axis=-1, keepdims=True) for i in each]
        gs = [(probs[i] * (grad_probs[i] - inner[i]) * 0.125).astype(bf16) for i in each]
        low = [dot(jnp.concatenate([gs[i], gs[i].T], axis=0), swapped[i][0], NN) for i in each]
        high = [dot(jnp.concatenate([probs_b[i].T, probs_b[i]], axis=0), swapped[i][1], NN) for i in each]
        for i in each:
            G[h, which[i], :, :128] = jnp.where(left, low[i][:CELLS], low[i][CELLS:]).astype(bf16)
            G[h, which[i], :, 128:] = jnp.where(left, high[i][:CELLS], high[i][CELLS:]).astype(bf16)

    def edge_copy(h):
        return remote(edge.at[h], edge_in.at[h], es.at[h], er.at[h], up)

    def attend(h):
        halo_copy(h).wait_recv()
        windows(h, list(range(MEMBERS)))
        edge[h] = dot(roll_from[:, :CELLS], G[h, MEMBERS - 1], NN).astype(bf16)
        edge_copy(h).start()
        for t in range(1, MEMBERS):
            U[h, t] = dot(roll_from[...], G[h, t - 1 : t + 1].reshape(2 * CELLS, 256), NN).astype(bf16)

    order = [3 - 3 * (z // 2), 2 - z // 2, (5 - z) % 4, z]

    left_p = lax.broadcasted_iota(jnp.int32, (plane, 128), 1) < 64

    def finish_cells(h):
        edge_copy(h).wait_recv()
        own = dot(roll_from[:, CELLS:], G[h, 0], NN)
        U[h, 0] = (own + edge_in[h].astype(f32)).astype(bf16)

    def far_cells(h):
        return remote(U.at[h], far_u.at[h], fus.at[h], fur.at[h], jnp.where(z == 0, up, down))

    def near_grads(h, i):
        d = order[i]
        cells = U[h].reshape(MEMBERS * CELLS, 256)
        rows = pl.ds(pl.multiple_of(d * plane, plane), plane)
        first = dot(XT[0, rows, :], cells, NN)
        second = dot(XT[1, rows, :], cells[:, 128:], NN)
        gW[h, d, :, :128] = first[:, :128].astype(bf16)
        gW[h, d, :, 128:] = jnp.where(left_p, first[:, 128:], second).astype(bf16)

    def far_grads(h):
        far_cells(h).wait_recv()
        cells = U[h].reshape(MEMBERS * CELLS, 256)
        more = far_u[h].reshape(MEMBERS * CELLS, 256)
        for i in range(2):
            d = order[i]
            rows = pl.ds(pl.multiple_of(d * plane, plane), plane)
            there = pl.ds(pl.multiple_of((d % 2) * plane, plane), plane)
            first = dot(XT[0, rows, :], cells, NN) + dot(far_xt[0, there, :], more, NN)
            second = dot(XT[1, rows, :], cells[:, 128:], NN) + dot(far_xt[1, there, :], more[:, 128:], NN)
            gW[h, d, :, :128] = first[:, :128].astype(bf16)
            gW[h, d, :, 128:] = jnp.where(left_p, first[:, 128:], second).astype(bf16)
            pl.when(z == 1)(lambda: z_copy(h, d, 0).start())
            pl.when(z == 2)(lambda: z_copy(h, d, 1).start())

    def z_copy(h, d, way):
        return remote(gW.at[h, d], zbuf.at[h, d, way], zs_s.at[h, d], zs_r.at[h, d, way],
                      up if way == 0 else down)

    def end_send(h, i):
        pl.when(z == 0)(lambda: z_copy(h, order[i], 0).start())
        pl.when(z == last)(lambda: z_copy(h, order[i], 1).start())

    def add(h, d, *ways):
        total = gW[h, d].astype(f32)
        for way in ways:
            total += zbuf[h, d, way].astype(f32)
        gW[h, d] = total.astype(bf16)

    def final_copy(h, k):
        to = (m + k) % 4
        rows = pl.ds(pl.multiple_of(to * depth, depth), depth)
        return remote(gW.at[h, z, rows], F.at[h, m], gs_s.at[h, k - 1], gs_r.at[h, k - 1], 4 * z + to)

    def line_step(h, i):
        d = order[i]

        def go_up():
            z_copy(h, d, 0).wait_recv()
            add(h, d, 0)
            z_copy(h, d, 0).start()

        def go_down():
            z_copy(h, d, 1).wait_recv()
            add(h, d, 1)
            z_copy(h, d, 1).start()

        if i < last:
            pl.when(middle & (d > z))(go_up)
            pl.when(middle & (d < z))(go_down)
            return

        def from_below():
            z_copy(h, d, 0).wait_recv()
            add(h, d, 0)

        def from_above():
            z_copy(h, d, 1).wait_recv()
            add(h, d, 1)
        pl.when(z > 0)(from_below)
        pl.when(z < last)(from_above)
        for k in (2, 1, 3):
            final_copy(h, k).start()
        F[h, m] = gW[h, z, pl.ds(pl.multiple_of(m * depth, depth), depth), :]

    def results(core, put):
        left_two = lax.broadcasted_iota(jnp.int32, (2 * CELLS, 128), 1) < 64

        def chunk(i, _):
            cols = pl.ds(pl.multiple_of(i * plane, plane), plane)
            attended = jnp.zeros((2 * CELLS, plane), f32)
            normed = jnp.zeros((2 * CELLS, plane), f32)
            for h in range(MINE):
                cells = jnp.concatenate([U[h, core], U[h, 2 + core]], axis=0)
                zero = jnp.zeros((2 * CELLS, 128), bf16)
                low, high = cells[:, :128], cells[:, 128:]
                w = W[h, pl.ds(i, 1)].reshape(plane, 256)
                attended += dot(jnp.where(left_two, zero, high), w[:, 128:], NT)
                values = jnp.concatenate([low, jnp.where(left_two, high, zero)], axis=1)
                normed += dot(values, w, NT)
            put(cols, (attended, normed))
            return 0
        lax.fori_loop(0, model // plane, chunk, 0)

    def core_copy():
        return remote(core_out, core_in, cs, cr, 4 * z + partner)

    def y_copy():
        return remote(y_out, y_in, ys, yr, 4 * z + across)

    def put_out(cols, both):
        for f in range(2):
            for yy in range(2):
                core_out[f, yy, :, cols] = both[f][yy * CELLS : (yy + 1) * CELLS].astype(bf16)

    def put_kept(cols, both):
        for f in range(2):
            for yy in range(2):
                kept[f, yy, :, cols] = both[f][yy * CELLS : (yy + 1) * CELLS]

    def assemble(h):
        for k in (2, 1, 3):
            final_copy(h, k).wait_recv()
        for member in range(MEMBERS):
            for block in range(4):
                at = block * width + 64 * (MINE * member + h)
                out[:, at : at + 64] = F[h, member, :, 64 * block : 64 * block + 64].astype(f32) * factor

    def finish_fields():
        y_copy().wait_recv()
        done = [(kept[f, y] + core_in[f, y].astype(f32) + y_in[f].astype(f32)).astype(bf16) for f in range(2)]
        if lats > 1:
            for f in range(2):
                outs[0][f] = done[f]
        else:
            outs[0][...] = (stream[...].astype(f32) + done[0].astype(f32)).astype(bf16)
            grad_stream = normalize_back(stream[...], gain[...].reshape(1, model), done[1])
            outs[1][...] = (cot[...].astype(f32) + grad_stream).astype(bf16)

    ends = jnp.logical_not(middle)

    def send_cells(h):
        finish_cells(h)
        pl.when(ends)(lambda: far_cells(h).start())

    def near(h):
        near_grads(h, 2)
        end_send(h, 2)
        near_grads(h, 3)

    project(0)
    weights_arrived(3, 2)
    project(1)
    attend(0)
    pl.when(middle)(far_first)
    project(2)
    attend(1)
    attend(2)
    pl.when(middle)(far_second)
    send_cells(0)
    send_cells(1)
    send_cells(2)
    results(1 - c, put_out)
    core_copy().start()
    near(0)
    results(c, put_kept)
    core_copy().wait_recv()
    for f in range(2):
        y_out[f] = (kept[f, 1 - y] + core_in[f, 1 - y].astype(f32)).astype(bf16)
    y_copy().start()
    pl.when(middle)(lambda: far_grads(0))
    near(1)
    pl.when(middle)(lambda: far_grads(1))
    near(2)
    pl.when(middle)(lambda: far_grads(2))
    line_step(0, 2)
    line_step(0, 3)
    line_step(1, 2)
    line_step(1, 3)
    assemble(0)
    finish_fields()
    line_step(2, 2)
    assemble(1)
    line_step(2, 3)
    assemble(2)

    for h in range(MINE):
        wp_copy(h).wait_send()
        wy_all(h, sent)
        wx_copy(h, z, x, True).wait_send()
        for k in (2, 1, 3):
            final_copy(h, k).wait_send()
        spread(h, z, sent, True, True)
        halo_copy(h).wait_send()
        edge_copy(h).wait_send()
        z_copy(h, order[2], 0).wait_send()

        def far_sent():
            for i in range(2):
                z_copy(h, order[i], 0).wait_send()
        pl.when(middle)(far_sent)
        pl.when(ends)(lambda: far_cells(h).wait_send())

    def weights_sent(zs, ways):
        for h in range(MINE):
            spread(h, zs, sent, **ways)
            wx_copy(h, zs, x).wait_send()

    for t in range(1, last + 1):
        from_planes(t, weights_sent)
    for f in range(2):
        for way in range(2):
            token_copy(f, way).wait_send()
        token_forward(f).wait_send()
    def far_moved():
        for f in range(2):
            far_y(f).wait_send()
            for which in range(2):
                far_pass(f, which).wait_send()
    for f in range(2):
        far_send(f, 0, sent)
    pl.when(middle)(far_moved)
    core_copy().wait_send()
    y_copy().wait_send()


def hand_over(*refs):
    count = len(refs) // 3
    copies = [pltpu.make_async_copy(refs[i], refs[count + i], refs[2 * count + i]) for i in range(count)]
    for copy in copies:
        copy.start()
    for copy in copies:
        copy.wait()


def on_device(tokens, land, surface, gain, weights, shifts, index_table, bias_table, cotangent):
    levels, tile_rows, tile_cols, model = tokens.shape
    width = weights.shape[1] // 4
    count = levels * tile_rows * tile_cols
    lats = lax.axis_size("lat")
    n = lax.axis_size("lon")
    depth = model // n
    dma = pltpu.SemaphoreType.DMA

    if lats > 1:
        surface_term = jnp.where(land[None, :, :, None] == 1, surface[1], surface[0])
        stream = (tokens.astype(f32) + surface_term).astype(bf16)
        fields = jnp.stack([normalize(stream, gain), cotangent])
        below = passed_along(fields, "lat", -1)
        both = jnp.concatenate([fields, below], axis=2)
        fields = take_rows(both, shifts[:, 0], tile_rows)
        given = (fields.reshape(2, count, model),)
        specs = [VMEM]
        results = [jax.ShapeDtypeStruct((2, count, model), bf16)]
    else:
        given = (tokens.reshape(count, model), cotangent.reshape(count, model), land, surface, gain)
        specs = [VMEM] * 5
        results = [jax.ShapeDtypeStruct((count, model), bf16)] * 2

    factor = 1.0 / math.sqrt(count * lats * n)
    plane = MEMBERS * depth
    last = n // MEMBERS
    vm = pltpu.VMEM
    *back, grad_weights = pl.pallas_call(
        functools.partial(layer_kernel, width, n, lats, factor),
        name="layer",
        out_shape=(
            *results,
            jax.ShapeDtypeStruct((depth, 4 * width), f32),
        ),
        in_specs=[VMEM] + specs + [SMEM, VMEM, SMEM],
        out_specs=(VMEM,) * (len(results) + 1),
        scratch_shapes=[
            vm((MINE, count, count), f32),
            vm((count, model), bf16),
            vm((2, MEMBERS, count, model // 2), bf16),
            vm((2, model // 2, MEMBERS * count), bf16),
            vm((MINE, MEMBERS, count, 256), bf16),
            dma((2, 2)), dma((2, 2)), dma((2, 2)), dma((2, 2)), dma((MINE,)), dma((MINE,)),
            vm((MEMBERS, MINE, depth, 256), bf16),
            vm((MINE, last, 2, 2, depth, 256), bf16),
            vm((2, MEMBERS, count, model), bf16),
            vm((2, model, MEMBERS * count), bf16),
            vm((MINE, MEMBERS + 1, count, 256), bf16),
            vm((MINE, MEMBERS, count, 256), bf16),
            vm((MINE, MEMBERS, count, 256), bf16),
            vm((MINE, count, 256), bf16),
            vm((MINE, count, 256), bf16),
            vm((MINE, last, plane, 256), bf16),
            vm((MINE, last, 2, plane, 256), bf16),
            vm((MINE, MEMBERS, depth, 256), bf16),
            vm((2, 2, count, model), f32),
            vm((2, 2, count, model), bf16),
            vm((2, 2, count, model), bf16),
            vm((2, count, model), bf16),
            vm((2, count, model), bf16),
            vm((count, 2 * count), bf16),
            vm((count, 2 * count), bf16),
            dma((MINE,)), dma((MINE,)), dma((MINE, 2)), dma((MINE,)),
            dma((MINE, last, 2)), dma((MINE, last)),
            dma((MINE, last)), dma((MINE, last)),
            dma((2, 2)), dma((2, 2)), dma((2,)), dma((2,)),
            dma((MINE,)), dma((MINE,)), dma((MINE,)), dma((MINE,)),
            dma((MINE, last)), dma((MINE, last, 2)),
            dma((MINE, 3)), dma((MINE, 3)),
            dma, dma, dma, dma,
        ],
        compiler_params=pltpu.CompilerParams(
            collective_id=0, has_side_effects=True, vmem_limit_bytes=60 * 2**20
        ),
        cost_estimate=pl.CostEstimate(flops=8 * 10**9, bytes_accessed=10 * 10**6, transcendentals=200000),
    )(weights, *given, bias_table.transpose(2, 0, 1), index_table, shifts)
    if lats == 1:
        made = (*back, grad_weights)
        made = pl.pallas_call(
            hand_over,
            name="hand_over",
            out_shape=tuple(jax.ShapeDtypeStruct(a.shape, a.dtype) for a in made),
            in_specs=[VMEM] * 3,
            out_specs=(ANY,) * 3,
            scratch_shapes=[dma] * 3,
            cost_estimate=pl.CostEstimate(flops=0, bytes_accessed=4 * 10**6, transcendentals=0),
        )(*made)
        return (made[0].reshape(tokens.shape), made[1].reshape(tokens.shape), made[2])
    back = back[0].reshape(2, levels, tile_rows, tile_cols, model)
    above = passed_along(back, "lat", 1)
    both = jnp.concatenate([above, back], axis=2)
    back = take_rows(both, tile_rows - shifts[:, 0], tile_rows)
    output = (stream.astype(f32) + back[0].astype(f32)).astype(bf16)
    grad_stream = normalize_back(stream, gain, back[1])
    grad_tokens = (cotangent.astype(f32) + grad_stream).astype(bf16)
    return (output, grad_tokens, lax.psum(grad_weights, "lat"))


def solution(mesh):
    return jax.shard_map(
        on_device,
        mesh=mesh,
        in_specs=(
            P("grp", "lat", "lon", None),
            P(("grp", "lat"), "lon"),
            P(),
            P(),
            P("lon", None),
            P(),
            P(),
            P("lat", None, None),
            P("grp", "lat", "lon", None),
        ),
        out_specs=(
            P("grp", "lat", "lon", None),
            P("grp", "lat", "lon", None),
            P(("grp", "lon"), None),
        ),
        check_vma=False,
    )
```

```python
import functools
import math

import jax
import jax.numpy as jnp
from jax import lax
from jax.experimental import pallas as pl
from jax.experimental.pallas import tpu as pltpu
from jax.sharding import PartitionSpec as P

epsilon = 1e-05
f32 = jnp.float32
bf16 = jnp.bfloat16
MESH = pl.DeviceIdType.MESH
ANY = pl.BlockSpec(memory_space=pl.ANY)
VMEM = pl.BlockSpec(memory_space=pltpu.VMEM)
SMEM = pl.BlockSpec(memory_space=pltpu.SMEM)
MEMBERS = 4
CELLS = 128
MINE = 3


def passed_along(shard, axis, by):
    count = lax.axis_size(axis)
    return lax.ppermute(shard, axis, [(i, (i + by) % count) for i in range(count)])


def dot(a, b, dims):
    return lax.dot_general(a, b, ((dims[0], dims[1]), ((), ())), preferred_element_type=f32)


NN = ((1,), (0,))
NT = ((1,), (1,))
TN = ((0,), (0,))


def normalize(stream, gain):
    values = stream.astype(f32)
    center = values - jnp.mean(values, axis=-1, keepdims=True)
    spread = lax.rsqrt(jnp.mean(center * center, axis=-1, keepdims=True) + epsilon)
    return (center * spread * gain).astype(bf16)


def normalize_back(stream, gain, grad_normed):
    values = stream.astype(f32)
    center = values - jnp.mean(values, axis=-1, keepdims=True)
    spread = lax.rsqrt(jnp.mean(center * center, axis=-1, keepdims=True) + epsilon)
    scaled = center * spread
    upstream = grad_normed.astype(f32) * gain
    return spread * (
        upstream
        - jnp.mean(upstream, axis=-1, keepdims=True)
        - scaled * jnp.mean(upstream * scaled, axis=-1, keepdims=True)
    )


def take_rows(both, starts, length):
    taken = both[:, :, :length]
    for start in range(1, length + 1):
        here = (starts == start)[None, :, None, None, None]
        taken = jnp.where(here, both[:, :, start : start + length], taken)
    return taken


def layer_kernel(width, n, lats, factor, *refs):
    if lats > 1:
        w_own, fields, table, index, shifts, *refs = refs
        outs, refs = refs[:2], refs[2:]
    else:
        w_own, tokens, cot, land, surface, gain, table, index, shifts, *refs = refs
        outs, refs = refs[:3], refs[3:]
    (bias, stream, far_x, far_xt, far_u, fxs, fxr, fps, fpr, fus, fur,
                 wown, W, X, XT, proj, G, U, edge, edge_in, gW, zbuf, F,
                 kept, core_out, core_in, y_out, y_in, roll_to, roll_from,
                 wps, wpr, wys, wyr, wzs, wzr, wxs, wxr, ts, tr, fs, fr, hs, hr, es, er,
                 zs_s, zs_r, gs_s, gs_r, cs, cr, ys, yr) = refs
    out = outs[-1]
    me = lax.axis_index("lon")
    x = lax.axis_index("grp")
    z, m = me // 4, me % 4
    y, c = m // 2, m % 2
    last = n // 4 - 1
    depth = w_own.shape[0]
    model = depth * n
    plane = 4 * depth
    partner, across = 2 * y + 1 - c, 2 * (1 - y) + c
    diag = 3 - m
    up, down = (me + 4) % n, (me + n - 4) % n

    def remote(src, dst, ssem, rsem, lon):
        return pltpu.make_async_remote_copy(
            src, dst, ssem, rsem, device_id={"lon": lon}, device_id_type=MESH)

    barrier = pltpu.get_barrier_semaphore()
    for k in range(1, 4):
        pl.semaphore_signal(barrier, inc=1, device_id={"lon": 4 * z + (m + k) % 4}, device_id_type=MESH)
    for lon in (up, down):
        pl.semaphore_signal(barrier, inc=1, device_id={"lon": lon}, device_id_type=MESH)
    pl.semaphore_signal(barrier, inc=1, device_id={"grp": 1 - x}, device_id_type=MESH)

    left = lax.broadcasted_iota(jnp.int32, (CELLS, 128), 1) < 64
    left_d = lax.broadcasted_iota(jnp.int32, (depth, 128), 1) < 64

    for pair in range(2 * width // 256):
        for first in (0, 2):
            a = w_own[:, first * width + 128 * pair : first * width + 128 * pair + 128].astype(f32)
            b = w_own[:, (first + 1) * width + 128 * pair : (first + 1) * width + 128 * pair + 128].astype(f32)
            low = jnp.where(left_d, a, pltpu.roll(b, 64, 1)).astype(bf16)
            high = jnp.where(left_d, pltpu.roll(a, 64, 1), b).astype(bf16)
            for head, value in ((2 * pair, low), (2 * pair + 1, high)):
                wown[head // MINE, head % MINE, :, 64 * first : 64 * first + 128] = value
    for h in range(MINE):
        W[h, z, y, c] = wown[m, h]
    if lats > 1:
        for f in range(2):
            X[f, m] = fields[f]
    else:
        X[1, m] = cot[...]

    pl.semaphore_wait(barrier, 6)

    def wp_copy(h):
        return remote(wown.at[partner, h], W.at[h, z, y, c], wps.at[h], wpr.at[h], 4 * z + partner)

    def wy_copy(h, core):
        to = 2 * (1 - y) + core
        return remote(wown.at[to, h], W.at[h, z, y, c], wys.at[h, core], wyr.at[h], 4 * z + to)

    def token_copy(f, way):
        to = across if way == 0 else partner
        return remote(X.at[f, m], X.at[f, m], ts.at[f, way], tr.at[f, way], 4 * z + to)

    def token_forward(f):
        return remote(X.at[f, across], X.at[f, across], fs.at[f], fr.at[f], 4 * z + partner)

    def wz_copy(h, zs, way):
        block = W.at[h, zs, :, x]
        to = up if way == 0 else down
        return remote(block, block, wzs.at[h, zs, way], wzr.at[h, zs], to)

    def wx_copy(h, zs, xx, here=False):
        block = W.at[h, zs, 1 - y, xx] if here else W.at[h, zs, :, xx]
        return pltpu.make_async_remote_copy(
            block, block, wxs.at[h, zs], wxr.at[h, zs], device_id={"grp": 1 - x}, device_id_type=MESH)

    def wy_all(h, act):
        def both():
            for core in range(2):
                act(wy_copy(h, core))
        pl.when(c == x)(both)

    start = lambda copy: copy.start()
    sent = lambda copy: copy.wait_send()
    for h in range(MINE):
        wp_copy(h).start()
        wy_all(h, start)
    for way in range(2):
        token_copy(1, way).start()
    if lats == 1:
        place = lax.broadcasted_iota(jnp.int32, (CELLS, 8), 0)
        spot = lax.broadcasted_iota(jnp.int32, (CELLS, 8), 1)
        row_hit = jnp.where(((place >> 3) & 7) == spot, 1.0, 0.0)
        marks = jnp.where((place & 7) == spot, dot(row_hit, land[...].astype(f32), NN), 0.0)
        on_land = jnp.sum(marks, axis=-1, keepdims=True) > 0.5
        term = jnp.where(on_land, surface[1:2, :], surface[0:1, :])
        stream[...] = (tokens[...].astype(f32) + term).astype(bf16)
        X[0, m] = normalize(stream[...], gain[...].reshape(1, model))
    for way in range(2):
        token_copy(0, way).start()

    lane = lax.broadcasted_iota(jnp.int32, (CELLS, 2 * CELLS), 1)
    cell = lax.broadcasted_iota(jnp.int32, (CELLS, 2 * CELLS), 0)

    def source(window_cell):
        lev, row, col = window_cell >> 6, (window_cell >> 3) & 7, window_cell & 7
        from_row = row
        if lats == 1:
            from_row = (row + jnp.where(lev == 0, shifts[0, 0], shifts[1, 0])) & 7
        from_col = col + jnp.where(lev == 0, shifts[0, 1], shifts[1, 1])
        return lev * 64 + from_row * 8 + (from_col & 7), from_col >= 8

    src, east = source(cell)
    roll_to[...] = jnp.where(src + jnp.where(east, CELLS, 0) == lane, 1.0, 0.0).astype(bf16)
    src, east = source(lane & 127)
    hit = (src == cell) & (jnp.where(east, 1, 0) == jnp.where(lane < CELLS, 1, 0))
    roll_from[...] = jnp.where(hit, 1.0, 0.0).astype(bf16)

    def spread(h, zs, act, to_up, to_down):
        if to_up:
            pl.when(z < last)(lambda: act(wz_copy(h, zs, 0)))
        if to_down:
            pl.when(z > 0)(lambda: act(wz_copy(h, zs, 1)))


    def transpose(t):
        for f in range(2):
            def chunk(i, _):
                cols = pl.ds(pl.multiple_of(i * 512, 512), 512)
                XT[f, cols, pl.ds(pl.multiple_of(t * CELLS, CELLS), CELLS)] = (
                    X[f, t, :, cols].astype(f32).T.astype(bf16))
                return 0
            lax.fori_loop(0, model // 512, chunk, 0)

    def from_planes(t, act):
        pl.when(z - t >= 0)(lambda: act(z - t, dict(to_up=True, to_down=False)))
        pl.when(z + t <= last)(lambda: act(z + t, dict(to_up=False, to_down=True)))

    def make_bias():
        area = CELLS // 2
        half = lax.broadcasted_iota(jnp.int32, (area, CELLS), 1) < area
        entry = jnp.concatenate([index[...], index[...]], axis=1)
        unroll = next(u for u in (5, 3, 1) if table.shape[2] % u == 0)

        def some(i, found):
            for u in range(unroll):
                r = i * unroll + u
                here = entry == r
                found = tuple(
                    jnp.where(here, jnp.where(half, table[MINE * m + h, 0, r], table[MINE * m + h, 1, r]), found[h])
                    for h in range(MINE))
            return found

        found = lax.fori_loop(
            0, table.shape[2] // unroll, some, tuple(jnp.zeros((area, CELLS), f32) for _ in range(MINE)))
        query = lax.broadcasted_iota(jnp.int32, (area, CELLS), 0) >> 3
        key = (lax.broadcasted_iota(jnp.int32, (area, CELLS), 1) & 63) >> 3
        first_row = 0 if lats == 1 else 8 * lax.axis_index("lat")
        for lev in range(2):
            edge_row = 8 * lats - shifts[lev, 0] - first_row
            same = jnp.where(query >= edge_row, 1, 0) == jnp.where(key >= edge_row, 1, 0)
            keep = half if lev == 0 else jnp.logical_not(half)
            for h in range(MINE):
                masked = jnp.where(same, found[h], -1e30)
                bias[h, lev * area : (lev + 1) * area, :] = jnp.where(keep, masked, -jnp.inf)

    def weights_arrived(t, h):
        if t == 0:
            wp_copy(h).wait_recv()
            wy_copy(h, 0).wait_recv()
            spread(h, z, start, True, True)
            wx_copy(h, z, x, True).start()
            return

        def arrived(zs, ways):
            wz_copy(h, zs, 0).wait_recv()
            spread(h, zs, start, **ways)
            wx_copy(h, zs, x).start()
        from_planes(t, arrived)

    half_model = model // 2
    middle = (z > 0) & (z < last)

    def far_tile(which):
        return m if which == 0 else across

    def far_copy(f, which, bottom):
        t = far_tile(which)
        cols = pl.ds(half_model if bottom else 0, half_model)
        return remote(X.at[f, t, :, cols], far_x.at[f, t], fxs.at[f, which], fxr.at[f, which], up if bottom else down)

    def far_send(f, which, act):
        pl.when(z == 0)(lambda: act(far_copy(f, which, True)))
        pl.when(z == last)(lambda: act(far_copy(f, which, False)))

    def far_pass(f, which):
        block = far_x.at[f, far_tile(which)]
        return remote(block, block, fps.at[f, which], fpr.at[f, which], 4 * z + partner)

    def far_transpose(f, t):
        for i in range(model // 2 // 256):
            rows = pl.ds(i * 256, 256)
            far_xt[f, rows, pl.ds(pl.multiple_of(t * CELLS, CELLS), CELLS)] = (
                far_x[f, t, :, rows].astype(f32).T.astype(bf16))

    def far_y(f):
        return remote(far_x.at[f, m], far_x.at[f, m], fxs.at[f, 1], fxr.at[f, 1], 4 * z + across)

    def far_own():
        for f in (1, 0):
            far_copy(f, 0, True).wait_recv()
            far_pass(f, 0).start()
            far_y(f).start()

    def far_first():
        for f in (1, 0):
            far_transpose(f, m)
        for f in (1, 0):
            far_pass(f, 0).wait_recv()
            far_transpose(f, partner)

    def far_second():
        for f in (1, 0):
            far_y(f).wait_recv()
            far_pass(f, 1).start()
            far_transpose(f, across)
        for f in (1, 0):
            far_pass(f, 1).wait_recv()
            far_transpose(f, diag)

    def tokens_across(f):
        token_copy(f, 0).wait_recv()
        token_forward(f).start()

    weights_arrived(0, 0)
    weights_arrived(1, 0)
    weights_arrived(0, 1)
    transpose(m)
    weights_arrived(2, 0)
    weights_arrived(1, 1)
    weights_arrived(0, 2)
    for f in (1, 0):
        far_send(f, 0, start)
    make_bias()
    for f in range(2):
        token_copy(f, 1).wait_recv()
    transpose(partner)
    weights_arrived(3, 0)
    tokens_across(1)
    weights_arrived(2, 1)
    weights_arrived(1, 2)
    weights_arrived(3, 1)
    tokens_across(0)
    pl.when(middle)(far_own)
    weights_arrived(2, 2)
    transpose(across)
    for f in range(2):
        token_forward(f).wait_recv()
    transpose(diag)

    def halo_copy(h):
        return remote(proj.at[h, 0], proj.at[h, MEMBERS], hs.at[h], hr.at[h], down)

    left_all = lax.broadcasted_iota(jnp.int32, (MEMBERS * CELLS, 128), 1) < 64

    def project(h):
        def wait_x(zs, ways):
            wx_copy(h, zs, 1 - x).wait_recv()
        wx_copy(h, z, 1 - x, True).wait_recv()
        for t in range(1, last + 1):
            from_planes(t, wait_x)
        w = W[h].reshape(model, 256)
        normed = dot(X[0].reshape(MEMBERS * CELLS, model), w, NN)
        grads = dot(X[1].reshape(MEMBERS * CELLS, model), w[:, 128:], NN)
        high = jnp.where(left_all, normed[:, 128:], grads)
        proj[h, :MEMBERS, :, :128] = normed[:, :128].astype(bf16).reshape(MEMBERS, CELLS, 128)
        proj[h, :MEMBERS, :, 128:] = high.astype(bf16).reshape(MEMBERS, CELLS, 128)
        halo_copy(h).start()

    def windows(h, which):
        each = range(len(which))
        zero = jnp.zeros((CELLS, 128), bf16)
        rolled = [dot(roll_to[...], proj[h, w : w + 2].reshape(2 * CELLS, 256), NN) for w in which]
        swapped = [(pltpu.roll(r[:, :128], 64, 1).astype(bf16), pltpu.roll(r[:, 128:], 64, 1).astype(bf16)) for r in rolled]
        q = [jnp.where(left, r[:, :128].astype(bf16), zero) for r in rolled]
        g = [jnp.where(left, zero, r[:, 128:].astype(bf16)) for r in rolled]
        kv = [jnp.where(left, kq, gv) for kq, gv in swapped]
        both = [dot(jnp.concatenate([q[i], g[i]], axis=0), kv[i], NT) for i in each]
        s = [a[:CELLS] * 0.125 + bias[h] for a in both]
        grad_probs = [a[CELLS:] for a in both]
        top = [jnp.max(a, axis=-1, keepdims=True) for a in s]
        expo = [jnp.exp(s[i] - top[i]) for i in each]
        share = [1.0 / jnp.sum(a, axis=-1, keepdims=True) for a in expo]
        probs = [expo[i] * share[i] for i in each]
        probs_b = [a.astype(bf16) for a in probs]
        inner = [jnp.sum(probs[i] * grad_probs[i], axis=-1, keepdims=True) for i in each]
        gs = [(probs[i] * (grad_probs[i] - inner[i]) * 0.125).astype(bf16) for i in each]
        low = [dot(jnp.concatenate([gs[i], gs[i].T], axis=0), swapped[i][0], NN) for i in each]
        high = [dot(jnp.concatenate([probs_b[i].T, probs_b[i]], axis=0), swapped[i][1], NN) for i in each]
        for i in each:
            G[h, which[i], :, :128] = jnp.where(left, low[i][:CELLS], low[i][CELLS:]).astype(bf16)
            G[h, which[i], :, 128:] = jnp.where(left, high[i][:CELLS], high[i][CELLS:]).astype(bf16)

    def edge_copy(h):
        return remote(edge.at[h], edge_in.at[h], es.at[h], er.at[h], up)

    def attend(h):
        halo_copy(h).wait_recv()
        windows(h, list(range(MEMBERS)))
        edge[h] = dot(roll_from[:, :CELLS], G[h, MEMBERS - 1], NN).astype(bf16)
        edge_copy(h).start()
        for t in range(1, MEMBERS):
            U[h, t] = dot(roll_from[...], G[h, t - 1 : t + 1].reshape(2 * CELLS, 256), NN).astype(bf16)

    order = [3 - 3 * (z // 2), 2 - z // 2, (5 - z) % 4, z]

    left_p = lax.broadcasted_iota(jnp.int32, (plane, 128), 1) < 64

    def finish_cells(h):
        edge_copy(h).wait_recv()
        own = dot(roll_from[:, CELLS:], G[h, 0], NN)
        U[h, 0] = (own + edge_in[h].astype(f32)).astype(bf16)

    def far_cells(h):
        return remote(U.at[h], far_u.at[h], fus.at[h], fur.at[h], jnp.where(z == 0, up, down))

    def near_grads(h, i):
        d = order[i]
        cells = U[h].reshape(MEMBERS * CELLS, 256)
        rows = pl.ds(pl.multiple_of(d * plane, plane), plane)
        first = dot(XT[0, rows, :], cells, NN)
        second = dot(XT[1, rows, :], cells[:, 128:], NN)
        gW[h, d, :, :128] = first[:, :128].astype(bf16)
        gW[h, d, :, 128:] = jnp.where(left_p, first[:, 128:], second).astype(bf16)

    def far_grads(h):
        far_cells(h).wait_recv()
        cells = U[h].reshape(MEMBERS * CELLS, 256)
        more = far_u[h].reshape(MEMBERS * CELLS, 256)
        for i in range(2):
            d = order[i]
            rows = pl.ds(pl.multiple_of(d * plane, plane), plane)
            there = pl.ds(pl.multiple_of((d % 2) * plane, plane), plane)
            first = dot(XT[0, rows, :], cells, NN) + dot(far_xt[0, there, :], more, NN)
            second = dot(XT[1, rows, :], cells[:, 128:], NN) + dot(far_xt[1, there, :], more[:, 128:], NN)
            gW[h, d, :, :128] = first[:, :128].astype(bf16)
            gW[h, d, :, 128:] = jnp.where(left_p, first[:, 128:], second).astype(bf16)
            pl.when(z == 1)(lambda: z_copy(h, d, 0).start())
            pl.when(z == 2)(lambda: z_copy(h, d, 1).start())

    def z_copy(h, d, way):
        return remote(gW.at[h, d], zbuf.at[h, d, way], zs_s.at[h, d], zs_r.at[h, d, way],
                      up if way == 0 else down)

    def end_send(h, i):
        pl.when(z == 0)(lambda: z_copy(h, order[i], 0).start())
        pl.when(z == last)(lambda: z_copy(h, order[i], 1).start())

    def add(h, d, *ways):
        total = gW[h, d].astype(f32)
        for way in ways:
            total += zbuf[h, d, way].astype(f32)
        gW[h, d] = total.astype(bf16)

    def final_copy(h, k):
        to = (m + k) % 4
        rows = pl.ds(pl.multiple_of(to * depth, depth), depth)
        return remote(gW.at[h, z, rows], F.at[h, m], gs_s.at[h, k - 1], gs_r.at[h, k - 1], 4 * z + to)

    def line_step(h, i):
        d = order[i]

        def go_up():
            z_copy(h, d, 0).wait_recv()
            add(h, d, 0)
            z_copy(h, d, 0).start()

        def go_down():
            z_copy(h, d, 1).wait_recv()
            add(h, d, 1)
            z_copy(h, d, 1).start()

        if i < last:
            pl.when(middle & (d > z))(go_up)
            pl.when(middle & (d < z))(go_down)
            return

        def from_below():
            z_copy(h, d, 0).wait_recv()
            add(h, d, 0)

        def from_above():
            z_copy(h, d, 1).wait_recv()
            add(h, d, 1)
        pl.when(z > 0)(from_below)
        pl.when(z < last)(from_above)
        for k in (2, 1, 3):
            final_copy(h, k).start()
        F[h, m] = gW[h, z, pl.ds(pl.multiple_of(m * depth, depth), depth), :]

    def results(core, put):
        left_two = lax.broadcasted_iota(jnp.int32, (2 * CELLS, 128), 1) < 64

        def chunk(i, _):
            cols = pl.ds(pl.multiple_of(i * plane, plane), plane)
            attended = jnp.zeros((2 * CELLS, plane), f32)
            normed = jnp.zeros((2 * CELLS, plane), f32)
            for h in range(MINE):
                cells = jnp.concatenate([U[h, core], U[h, 2 + core]], axis=0)
                zero = jnp.zeros((2 * CELLS, 128), bf16)
                low, high = cells[:, :128], cells[:, 128:]
                w = W[h, pl.ds(i, 1)].reshape(plane, 256)
                attended += dot(jnp.where(left_two, zero, high), w[:, 128:], NT)
                values = jnp.concatenate([low, jnp.where(left_two, high, zero)], axis=1)
                normed += dot(values, w, NT)
            put(cols, (attended, normed))
            return 0
        lax.fori_loop(0, model // plane, chunk, 0)

    def core_copy():
        return remote(core_out, core_in, cs, cr, 4 * z + partner)

    def y_copy():
        return remote(y_out, y_in, ys, yr, 4 * z + across)

    def put_out(cols, both):
        for f in range(2):
            for yy in range(2):
                core_out[f, yy, :, cols] = both[f][yy * CELLS : (yy + 1) * CELLS].astype(bf16)

    def put_kept(cols, both):
        for f in range(2):
            for yy in range(2):
                kept[f, yy, :, cols] = both[f][yy * CELLS : (yy + 1) * CELLS]

    def assemble(h):
        for k in (2, 1, 3):
            final_copy(h, k).wait_recv()
        for member in range(MEMBERS):
            for block in range(4):
                at = block * width + 64 * (MINE * member + h)
                out[:, at : at + 64] = F[h, member, :, 64 * block : 64 * block + 64].astype(f32) * factor

    def finish_fields():
        y_copy().wait_recv()
        done = [(kept[f, y] + core_in[f, y].astype(f32) + y_in[f].astype(f32)).astype(bf16) for f in range(2)]
        if lats > 1:
            for f in range(2):
                outs[0][f] = done[f]
        else:
            outs[0][...] = (stream[...].astype(f32) + done[0].astype(f32)).astype(bf16)
            grad_stream = normalize_back(stream[...], gain[...].reshape(1, model), done[1])
            outs[1][...] = (cot[...].astype(f32) + grad_stream).astype(bf16)

    ends = jnp.logical_not(middle)

    def send_cells(h):
        finish_cells(h)
        pl.when(ends)(lambda: far_cells(h).start())

    def near(h):
        near_grads(h, 2)
        end_send(h, 2)
        near_grads(h, 3)

    project(0)
    weights_arrived(3, 2)
    project(1)
    attend(0)
    project(2)
    attend(1)
    pl.when(middle)(far_first)
    attend(2)
    pl.when(middle)(far_second)
    send_cells(0)
    send_cells(1)
    send_cells(2)
    results(1 - c, put_out)
    core_copy().start()
    near(0)
    results(c, put_kept)
    core_copy().wait_recv()
    for f in range(2):
        y_out[f] = (kept[f, 1 - y] + core_in[f, 1 - y].astype(f32)).astype(bf16)
    y_copy().start()
    pl.when(middle)(lambda: far_grads(0))
    pl.when(middle)(lambda: far_grads(1))
    near(1)
    line_step(0, 2)
    pl.when(middle)(lambda: far_grads(2))
    near(2)
    line_step(0, 3)
    line_step(1, 2)
    line_step(1, 3)
    assemble(0)
    finish_fields()
    line_step(2, 2)
    assemble(1)
    line_step(2, 3)
    assemble(2)

    for h in range(MINE):
        wp_copy(h).wait_send()
        wy_all(h, sent)
        wx_copy(h, z, x, True).wait_send()
        for k in (2, 1, 3):
            final_copy(h, k).wait_send()
        spread(h, z, sent, True, True)
        halo_copy(h).wait_send()
        edge_copy(h).wait_send()
        z_copy(h, order[2], 0).wait_send()

        def far_sent():
            for i in range(2):
                z_copy(h, order[i], 0).wait_send()
        pl.when(middle)(far_sent)
        pl.when(ends)(lambda: far_cells(h).wait_send())

    def weights_sent(zs, ways):
        for h in range(MINE):
            spread(h, zs, sent, **ways)
            wx_copy(h, zs, x).wait_send()

    for t in range(1, last + 1):
        from_planes(t, weights_sent)
    for f in range(2):
        for way in range(2):
            token_copy(f, way).wait_send()
        token_forward(f).wait_send()
    def far_moved():
        for f in range(2):
            far_y(f).wait_send()
            for which in range(2):
                far_pass(f, which).wait_send()
    for f in range(2):
        far_send(f, 0, sent)
    pl.when(middle)(far_moved)
    core_copy().wait_send()
    y_copy().wait_send()


def hand_over(*refs):
    given, outs, held = refs[:3], refs[3:6], refs[6:9]
    loads = [pltpu.make_async_copy(given[i], held[i], refs[9].at[i]) for i in range(3)]
    stores = [pltpu.make_async_copy(held[i], outs[i], refs[10].at[i]) for i in range(3)]
    for load in loads:
        load.start()
    for load, store in zip(loads, stores):
        load.wait()
        store.start()
    for store in stores:
        store.wait()


def on_device(tokens, land, surface, gain, weights, shifts, index_table, bias_table, cotangent):
    levels, tile_rows, tile_cols, model = tokens.shape
    width = weights.shape[1] // 4
    count = levels * tile_rows * tile_cols
    lats = lax.axis_size("lat")
    n = lax.axis_size("lon")
    depth = model // n
    dma = pltpu.SemaphoreType.DMA

    if lats > 1:
        surface_term = jnp.where(land[None, :, :, None] == 1, surface[1], surface[0])
        stream = (tokens.astype(f32) + surface_term).astype(bf16)
        fields = jnp.stack([normalize(stream, gain), cotangent])
        below = passed_along(fields, "lat", -1)
        both = jnp.concatenate([fields, below], axis=2)
        fields = take_rows(both, shifts[:, 0], tile_rows)
        given = (fields.reshape(2, count, model),)
        specs = [VMEM]
        results = [jax.ShapeDtypeStruct((2, count, model), bf16)]
    else:
        given = (tokens.reshape(count, model), cotangent.reshape(count, model), land, surface, gain)
        specs = [VMEM] * 5
        results = [jax.ShapeDtypeStruct((count, model), bf16)] * 2

    factor = 1.0 / math.sqrt(count * lats * n)
    plane = MEMBERS * depth
    last = n // MEMBERS
    vm = pltpu.VMEM
    *back, grad_weights = pl.pallas_call(
        functools.partial(layer_kernel, width, n, lats, factor),
        name="layer",
        out_shape=(
            *results,
            jax.ShapeDtypeStruct((depth, 4 * width), f32),
        ),
        in_specs=[VMEM] + specs + [SMEM, VMEM, SMEM],
        out_specs=(VMEM,) * (len(results) + 1),
        scratch_shapes=[
            vm((MINE, count, count), f32),
            vm((count, model), bf16),
            vm((2, MEMBERS, count, model // 2), bf16),
            vm((2, model // 2, MEMBERS * count), bf16),
            vm((MINE, MEMBERS, count, 256), bf16),
            dma((2, 2)), dma((2, 2)), dma((2, 2)), dma((2, 2)), dma((MINE,)), dma((MINE,)),
            vm((MEMBERS, MINE, depth, 256), bf16),
            vm((MINE, last, 2, 2, depth, 256), bf16),
            vm((2, MEMBERS, count, model), bf16),
            vm((2, model, MEMBERS * count), bf16),
            vm((MINE, MEMBERS + 1, count, 256), bf16),
            vm((MINE, MEMBERS, count, 256), bf16),
            vm((MINE, MEMBERS, count, 256), bf16),
            vm((MINE, count, 256), bf16),
            vm((MINE, count, 256), bf16),
            vm((MINE, last, plane, 256), bf16),
            vm((MINE, last, 2, plane, 256), bf16),
            vm((MINE, MEMBERS, depth, 256), bf16),
            vm((2, 2, count, model), f32),
            vm((2, 2, count, model), bf16),
            vm((2, 2, count, model), bf16),
            vm((2, count, model), bf16),
            vm((2, count, model), bf16),
            vm((count, 2 * count), bf16),
            vm((count, 2 * count), bf16),
            dma((MINE,)), dma((MINE,)), dma((MINE, 2)), dma((MINE,)),
            dma((MINE, last, 2)), dma((MINE, last)),
            dma((MINE, last)), dma((MINE, last)),
            dma((2, 2)), dma((2, 2)), dma((2,)), dma((2,)),
            dma((MINE,)), dma((MINE,)), dma((MINE,)), dma((MINE,)),
            dma((MINE, last)), dma((MINE, last, 2)),
            dma((MINE, 3)), dma((MINE, 3)),
            dma, dma, dma, dma,
        ],
        compiler_params=pltpu.CompilerParams(
            collective_id=0, has_side_effects=True, vmem_limit_bytes=60 * 2**20
        ),
        cost_estimate=pl.CostEstimate(flops=8 * 10**9, bytes_accessed=10 * 10**6, transcendentals=200000),
    )(weights, *given, bias_table.transpose(2, 0, 1), index_table, shifts)
    if lats == 1:
        made = (*back, grad_weights)
        made = pl.pallas_call(
            hand_over,
            name="hand_over",
            out_shape=tuple(jax.ShapeDtypeStruct(a.shape, a.dtype) for a in made),
            in_specs=[ANY] * 3,
            out_specs=(ANY,) * 3,
            scratch_shapes=[vm(a.shape, a.dtype) for a in made] + [dma((3,)), dma((3,))],
            cost_estimate=pl.CostEstimate(flops=0, bytes_accessed=4 * 10**6, transcendentals=0),
        )(*made)
        return (made[0].reshape(tokens.shape), made[1].reshape(tokens.shape), made[2])
    back = back[0].reshape(2, levels, tile_rows, tile_cols, model)
    above = passed_along(back, "lat", 1)
    both = jnp.concatenate([above, back], axis=2)
    back = take_rows(both, tile_rows - shifts[:, 0], tile_rows)
    output = (stream.astype(f32) + back[0].astype(f32)).astype(bf16)
    grad_stream = normalize_back(stream, gain, back[1])
    grad_tokens = (cotangent.astype(f32) + grad_stream).astype(bf16)
    return (output, grad_tokens, lax.psum(grad_weights, "lat"))


def solution(mesh):
    return jax.shard_map(
        on_device,
        mesh=mesh,
        in_specs=(
            P("grp", "lat", "lon", None),
            P(("grp", "lat"), "lon"),
            P(),
            P(),
            P("lon", None),
            P(),
            P(),
            P("lat", None, None),
            P("grp", "lat", "lon", None),
        ),
        out_specs=(
            P("grp", "lat", "lon", None),
            P("grp", "lat", "lon", None),
            P(("grp", "lon"), None),
        ),
        check_vma=False,
    )
```
